32 devices in a mesh: row: 8 (over z, x), col: 4 (over y, core).
Axes of the slice: x: 2, y: 2, z: 4, core: 2. Of those that a mesh axis runs over, the one named last changes fastest.
Arguments:
- tokens: bfloat16 [512, 8192], P('col', 'row'), may hold values from -6 to 6
- gate_weight: bfloat16 [8192, 14336], P('row', 'col'), may hold values from -0.09375 to 0.09375
- up_weight: bfloat16 [8192, 14336], P('row', 'col'), may hold values from -0.09375 to 0.09375
- down_weight: bfloat16 [14336, 8192], P('col', 'row'), may hold values from -0.09375 to 0.09375
- gate_mask: int32 [128, 224], P('row', 'col'), may hold values from 0 to 1, as said below
- up_mask: int32 [128, 224], P('row', 'col'), may hold values from 0 to 1, as said below
- down_mask: int32 [224, 128], P('col', 'row'), may hold values from 0 to 1, as said below
- head_weight: bfloat16 [8192, 128], P('row'), may hold values from -0.15625 to 0.15625
- labels: int32 [512], P('col'), may hold values from 0 to 127
Outputs:
- token_loss: float32 [512], P('col')
- tokens_grad: bfloat16 [512, 8192], P('col', 'row')
- gate_grad: bfloat16 [8192, 14336], P('row', 'col')
- up_grad: bfloat16 [8192, 14336], P('row', 'col')
- down_grad: bfloat16 [14336, 8192], P('col', 'row')
The draws below stay inside these ranges and needn't reach their ends.
Inputs may be any that keep to these rules, and one draw needn't show every extreme that they name: `gate_mask`: 1 keeps a block of 64 x 64 weights, 0 prunes it. `up_mask`: 1 keeps a block of 64 x 64 weights, 0 prunes it. `down_mask`: 1 keeps a block of 64 x 64 weights, 0 prunes it.
All inputs are finite; a program needn't handle non-finite values.
Results may differ from the reference program's by a relative error of at most 0.011.
Values may be sent and summed in bfloat16 or wider, within the bound.
A program may use at most 192 MiB of HBM per device.

```python
import jax
import jax.numpy as jnp
from jax import lax

D = 8192
FF = 14336
BLOCK = 64
CLASSES = 128
TOKENS = 512


def keep_blocks(key, height, breadth, by_rows):
    level_key, pick_key = jax.random.split(key)
    if by_rows:
        level = jax.random.randint(level_key, (height, 1), 1, 4)
    else:
        level = jax.random.randint(level_key, (1, breadth), 1, 4)
    picks = jax.random.randint(pick_key, (height, breadth), 0, 4)
    return (picks < level).astype(jnp.int32)


def draw_gate_mask(key, part):
    return keep_blocks(jax.random.fold_in(key, 11), D // BLOCK, FF // BLOCK, True)


def draw_up_mask(key, part):
    return keep_blocks(jax.random.fold_in(key, 23), D // BLOCK, FF // BLOCK, True)


def draw_down_mask(key, part):
    return keep_blocks(jax.random.fold_in(key, 37), FF // BLOCK, D // BLOCK, False)


def touch_ends(array, key, least, high):
    longest = array.shape.index(max(array.shape))
    spots = []
    for shift in (0, 1):
        where = [jax.random.randint(jax.random.fold_in(key, axis), (), 0, length) for axis, length in enumerate(array.shape)]
        where[longest] = (where[longest] + shift) % array.shape[longest]
        spots.append(tuple(where))
    return array.at[spots[0]].set(least).at[spots[1]].set(high)


def levels(own_key, shape, shards, low, largest):
    gain = 1.0
    for axis_at, parts in shards:
        steps = jax.random.uniform(jax.random.fold_in(jax.random.fold_in(own_key, 6), axis_at), (parts,), jnp.float32, low / len(shards), largest / len(shards))
        gain = gain * jnp.repeat(jnp.exp(steps), shape[axis_at] // parts).reshape((-1,) + (1,) * (len(shape) - 1 - axis_at))
    return gain


def noise(stream_key, dims, spread, reach, shards=(), held_as=jnp.bfloat16):
    gain = levels(stream_key, dims, shards, -0.22, 0.18) if shards else 1.0
    entries = jax.random.normal(stream_key, dims, jnp.float32) * spread * gain
    return jnp.minimum(jnp.maximum(entries, -reach), reach).astype(held_as)


def setup_inputs(seed: int = 0) -> dict:
    arg_keys = jax.random.split(jax.random.key(seed), 10)
    return {
        "tokens": noise(arg_keys[0], (TOKENS, D), 1.0, 6.0, ((0, 4), (1, 8))),
        "gate_weight": noise(arg_keys[1], (D, FF), (D // 2) ** -0.5, 0.09375, ((0, 8), (1, 4))),
        "up_weight": noise(arg_keys[2], (D, FF), (D // 2) ** -0.5, 0.09375, ((0, 8), (1, 4))),
        "down_weight": noise(arg_keys[3], (FF, D), (FF // 4) ** -0.5, 0.09375, ((0, 4), (1, 8))),
        "gate_mask": draw_gate_mask(jax.random.fold_in(arg_keys[9], 71), 0),
        "up_mask": draw_up_mask(jax.random.fold_in(arg_keys[9], 71), 0),
        "down_mask": draw_down_mask(jax.random.fold_in(arg_keys[9], 71), 0),
        "head_weight": noise(arg_keys[7], (D, CLASSES), (D // 6) ** -0.5, 0.15625, ((0, 8),)),
        "labels": touch_ends(jax.random.randint(arg_keys[8], (TOKENS,), 0, CLASSES), jax.random.fold_in(arg_keys[8], 1), 0, CLASSES - 1).astype(jnp.int32),
    }


loss_scale = 8.0


def masked(weight, block_mask):
    height, breadth = weight.shape
    blocks = weight.reshape(block_mask.shape[0], height // block_mask.shape[0], block_mask.shape[1], breadth // block_mask.shape[1])
    pruned = blocks * block_mask[:, None, :, None].astype(weight.dtype)
    return pruned.reshape(height, breadth)


def classify(logits, labels):
    exponent = jnp.exp(logits)
    partition = jnp.sum(exponent, axis=1, keepdims=True)
    classes = lax.broadcasted_iota(jnp.int32, logits.shape, 1)
    onehot = (labels[:, None] == classes).astype(jnp.float32)
    token_cost = jnp.log(partition[:, 0]) - jnp.sum(logits * onehot, axis=1)
    return token_cost, loss_scale * (exponent / partition - onehot)


def reference(tokens, gate_weight, up_weight, down_weight, gate_mask, up_mask, down_mask, head_weight, labels):
    gate_kept = masked(gate_weight, gate_mask)
    up_kept = masked(up_weight, up_mask)
    down_kept = masked(down_weight, down_mask)
    gate_sum = jnp.dot(tokens, gate_kept, preferred_element_type=jnp.float32)
    up_sum = jnp.dot(tokens, up_kept, preferred_element_type=jnp.float32)
    sigmoid_gate = jax.nn.sigmoid(gate_sum)
    activated = gate_sum * sigmoid_gate
    hidden = (activated * up_sum).astype(jnp.bfloat16)
    mixed_rows = (tokens.astype(jnp.float32) + jnp.dot(hidden, down_kept, preferred_element_type=jnp.float32)).astype(jnp.bfloat16)
    logits = jnp.dot(mixed_rows, head_weight, preferred_element_type=jnp.float32)
    token_loss, grad_full = classify(logits, labels)
    dlogits = grad_full.astype(jnp.bfloat16)
    dmixed = jnp.dot(dlogits, head_weight.T, preferred_element_type=jnp.float32).astype(jnp.bfloat16)
    dhidden = jnp.dot(dmixed, down_kept.T, preferred_element_type=jnp.float32)
    gate_delta = (dhidden * up_sum * sigmoid_gate * (1.0 + gate_sum * (1.0 - sigmoid_gate))).astype(jnp.bfloat16)
    up_delta = (dhidden * activated).astype(jnp.bfloat16)
    down_grad = masked(jnp.dot(hidden.T, dmixed, preferred_element_type=jnp.float32), down_mask).astype(jnp.bfloat16)
    gate_grad = masked(jnp.dot(tokens.T, gate_delta, preferred_element_type=jnp.float32), gate_mask).astype(jnp.bfloat16)
    up_grad = masked(jnp.dot(tokens.T, up_delta, preferred_element_type=jnp.float32), up_mask).astype(jnp.bfloat16)
    input_sum = jnp.dot(gate_delta, gate_kept.T, preferred_element_type=jnp.float32) + jnp.dot(up_delta, up_kept.T, preferred_element_type=jnp.float32)
    tokens_grad = (dmixed.astype(jnp.float32) + input_sum).astype(jnp.bfloat16)
    return (token_loss, tokens_grad, gate_grad, up_grad, down_grad)
```

```python
import functools

import jax
import jax.numpy as jnp
from jax import lax
from jax.experimental import pallas as pl
from jax.experimental.pallas import tpu as pltpu
from jax.sharding import PartitionSpec as P

loss_scale = 8.0
F32 = jnp.float32
BF16 = jnp.bfloat16
MESH = pl.DeviceIdType.MESH


def classify(logits, labels):
    exponent = jnp.exp(logits)
    partition = jnp.sum(exponent, axis=1, keepdims=True)
    classes = lax.broadcasted_iota(jnp.int32, logits.shape, 1)
    onehot = (labels[:, None] == classes).astype(F32)
    token_cost = jnp.log(partition[:, 0]) - jnp.sum(logits * onehot, axis=1)
    return (token_cost, loss_scale * (exponent / partition - onehot))


def tile_of(width):
    for tile in (512, 256, 128):
        if width % tile == 0:
            return tile
    return width


def widened(mask, width):
    return jnp.repeat(mask.astype(F32), width // mask.shape[1], axis=1)


def pruned(values, mask):
    height, breadth = values.shape
    blocks = mask.shape[0]
    split = values.reshape(blocks, height // blocks, breadth)
    kept = split * mask[:, None, :].astype(values.dtype)
    return kept.reshape(height, breadth)


def dot(a, b, a_axis, b_axis):
    return lax.dot_general(a, b, (((a_axis,), (b_axis,)), ((), ())), preferred_element_type=F32)


def run(body, grid, in_specs, out_specs, out_shape, flops, touched, scratch=()):
    return pl.pallas_call(
        body,
        grid=grid,
        in_specs=in_specs,
        out_specs=out_specs,
        out_shape=out_shape,
        scratch_shapes=list(scratch),
        compiler_params=pltpu.CompilerParams(vmem_limit_bytes=40 << 20),
        cost_estimate=pl.CostEstimate(flops=flops, bytes_accessed=touched, transcendentals=0),
    )


def gate_up_parts(x, gate, up, gate_mask, up_mask, rows):
    tokens, depth = x.shape
    width = gate.shape[1]
    tile = tile_of(width)
    blocks = gate_mask.shape[0]

    def body(x_ref, g_ref, u_ref, gm_ref, um_ref, o_ref):
        for k, (w, m) in enumerate(((g_ref, gm_ref), (u_ref, um_ref))):
            part = dot(x_ref[...], pruned(w[...], m[...]), 1, 0).astype(BF16)
            o_ref[:, k] = part.reshape(rows, tokens // rows, tile)

    weight = pl.BlockSpec((depth, tile), lambda j: (0, j))
    mask = pl.BlockSpec((blocks, tile), lambda j: (0, j))
    return run(
        body,
        (width // tile,),
        [pl.BlockSpec((tokens, depth), lambda j: (0, 0)), weight, weight, mask, mask],
        pl.BlockSpec((rows, 2, tokens // rows, tile), lambda j: (0, 0, 0, j)),
        jax.ShapeDtypeStruct((rows, 2, tokens // rows, width), BF16),
        4 * tokens * depth * width,
        4 * depth * width + 4 * tokens * width,
    )(x, gate, up, gate_mask, up_mask)


def head_part(down, mask, head):
    width, depth = down.shape
    classes = head.shape[1]
    tile = tile_of(width)
    steps = width // tile
    mask = mask.reshape(steps, -1, depth)

    def body(w_ref, m_ref, h_ref, o_ref):
        o_ref[...] = dot(pruned(w_ref[...], m_ref[0]), h_ref[...], 1, 0).astype(BF16)

    return run(
        body,
        (steps,),
        [
            pl.BlockSpec((tile, depth), lambda j: (j, 0)),
            pl.BlockSpec((1, mask.shape[1], depth), lambda j: (j, 0, 0)),
            pl.BlockSpec((depth, classes), lambda j: (0, 0)),
        ],
        pl.BlockSpec((tile, classes), lambda j: (j, 0)),
        jax.ShapeDtypeStruct((width, classes), BF16),
        2 * classes * depth * width,
        2 * depth * width,
    )(down, mask, head)


def backward(x, sums, dlogits, fold, head, gate, up, gate_mask, up_mask, down_mask):
    rows, _, share, width = sums.shape
    tokens, depth = x.shape
    classes = dlogits.shape[1]
    tile = tile_of(width)
    steps = width // tile
    blocks = gate_mask.shape[0]
    down_mask = down_mask.reshape(steps, -1, depth)

    def body(x_ref, s_ref, d_ref, f_ref, h_ref, g_ref, u_ref, gm_ref, um_ref, dm_ref, gg_ref, ug_ref, dg_ref, o_ref, mix_ref, acc, dmixed):
        j = pl.program_id(0)

        @pl.when(j == 0)
        def _():
            dmixed[...] = dot(d_ref[...], h_ref[...], 1, 1).astype(BF16)
            mix_ref[...] = dmixed[...]

        dhidden = dot(d_ref[...], f_ref[...], 1, 1)
        gate_sum = s_ref[:, 0].reshape(tokens, tile).astype(F32)
        up_sum = s_ref[:, 1].reshape(tokens, tile).astype(F32)
        sigmoid_gate = jax.nn.sigmoid(gate_sum)
        activated = gate_sum * sigmoid_gate
        hidden = (activated * up_sum).astype(BF16)
        gate_delta = (dhidden * up_sum * sigmoid_gate * (1.0 + gate_sum * (1.0 - sigmoid_gate))).astype(BF16)
        up_delta = (dhidden * activated).astype(BF16)
        gg_ref[...] = pruned(dot(x_ref[...], gate_delta, 0, 0), gm_ref[...]).astype(BF16)
        ug_ref[...] = pruned(dot(x_ref[...], up_delta, 0, 0), um_ref[...]).astype(BF16)
        dg_ref[...] = pruned(dot(hidden, dmixed[...], 0, 0), dm_ref[0]).astype(BF16)
        part = dot(gate_delta, pruned(g_ref[...], gm_ref[...]), 1, 1)
        part += dot(up_delta, pruned(u_ref[...], um_ref[...]), 1, 1)

        @pl.when(j == 0)
        def _():
            acc[...] = part

        @pl.when(j > 0)
        def _():
            acc[...] += part

        @pl.when(j == steps - 1)
        def _():
            o_ref[...] = acc[...].astype(BF16)

    weight = pl.BlockSpec((depth, tile), lambda j: (0, j))
    mask = pl.BlockSpec((blocks, tile), lambda j: (0, j))
    whole = lambda *shape: pl.BlockSpec(shape, lambda j: (0,) * len(shape))
    return run(
        body,
        (steps,),
        [
            whole(tokens, depth),
            pl.BlockSpec((rows, 2, share, tile), lambda j: (0, 0, 0, j)),
            whole(tokens, classes),
            pl.BlockSpec((tile, classes), lambda j: (j, 0)),
            whole(depth, classes),
            weight,
            weight,
            mask,
            mask,
            pl.BlockSpec((1, down_mask.shape[1], depth), lambda j: (j, 0, 0)),
        ],
        [weight, weight, pl.BlockSpec((tile, depth), lambda j: (j, 0)), whole(tokens, depth), whole(tokens, depth)],
        [
            jax.ShapeDtypeStruct((depth, width), BF16),
            jax.ShapeDtypeStruct((depth, width), BF16),
            jax.ShapeDtypeStruct((width, depth), BF16),
            jax.ShapeDtypeStruct((tokens, depth), BF16),
            jax.ShapeDtypeStruct((tokens, depth), BF16),
        ],
        10 * tokens * depth * width,
        10 * depth * width,
        [pltpu.VMEM((tokens, depth), F32), pltpu.VMEM((tokens, depth), BF16)],
    )(x, sums, dlogits, fold, head, gate, up, gate_mask, up_mask, down_mask)


def grid_of(axis, fast, size):
    me = lax.axis_index(axis)
    return me, lax.div(me, fast), lax.rem(me, fast), size // fast


def greet(axis, slow, quick, slows, fast):
    barrier = pltpu.get_barrier_semaphore()
    for d in range(1, fast):
        there = slow * fast + lax.rem(quick + d, fast)
        pl.semaphore_signal(barrier, inc=1, device_id={axis: there}, device_id_type=MESH)
    for d in range(1, slows):
        there = lax.rem(slow + d, slows) * fast + quick
        pl.semaphore_signal(barrier, inc=1, device_id={axis: there}, device_id_type=MESH)
    pl.semaphore_wait(barrier, fast + slows - 2)


def send(src, dst, sems, where, axis, there):
    copy = pltpu.make_async_remote_copy(
        src_ref=src,
        dst_ref=dst,
        send_sem=sems[0].at[where],
        recv_sem=sems[1].at[where],
        device_id={axis: there},
        device_id_type=MESH,
    )
    copy.start()
    return copy


def talking(call_id):
    return pltpu.CompilerParams(
        collective_id=call_id, has_side_effects=True, vmem_limit_bytes=56 << 20
    )


def both(*dims):
    return [pltpu.SemaphoreType.DMA(dims), pltpu.SemaphoreType.DMA(dims)]


def reduce_scatter(parts, axis, fast, slices, call_id):
    size, height, width = parts.shape
    slows = size // fast
    step = height // slices
    group = 16

    def body(p_ref, o_ref, xbuf, ybuf, zbuf, *sems):
        xsems, zsems = sems[:2], sems[2:]
        _, slow, quick, _ = grid_of(axis, fast, size)
        greet(axis, slow, quick, slows, fast)
        order = [(d, s) for s in range(slices) for d in [*range(1, slows), 0]]
        xcopies, zcopies = {}, {}
        for d, s in order:
            a = lax.rem(slow + d, slows)
            cut = pl.ds(s * step, step)
            for e in range(1, fast):
                b = lax.rem(quick + e, fast)
                xcopies[d, s, e] = send(
                    p_ref.at[a * fast + b, cut],
                    xbuf.at[e - 1, d, cut],
                    xsems,
                    (d * slices + s) * (fast - 1) + e - 1,
                    axis,
                    slow * fast + b,
                )
        for d, s in order:
            a = lax.rem(slow + d, slows)
            for e in range(1, fast):
                xcopies[d, s, e].wait_recv()

            def add(i, carry, d=d, s=s, a=a):
                at = pl.ds(pl.multiple_of(s * step + i * group, group), group)
                total = p_ref[a * fast + quick, at].astype(F32)
                for e in range(1, fast):
                    total += xbuf[e - 1, d, at].astype(F32)
                if d == 0:
                    o_ref[at] = total
                else:
                    ybuf[d - 1, at] = total.astype(BF16)
                return carry

            lax.fori_loop(0, step // group, add, 0)
            if d:
                cut = pl.ds(s * step, step)
                zcopies[d, s] = send(
                    ybuf.at[d - 1, cut],
                    zbuf.at[d - 1, cut],
                    zsems,
                    (d - 1) * slices + s,
                    axis,
                    a * fast + quick,
                )
        for s in range(slices):
            for d in range(1, slows):
                zcopies[d, s].wait_recv()

            def close(i, carry, s=s):
                at = pl.ds(pl.multiple_of(s * step + i * group, group), group)
                total = o_ref[at]
                for d in range(1, slows):
                    total += zbuf[d - 1, at].astype(F32)
                o_ref[at] = total
                return carry

            lax.fori_loop(0, step // group, close, 0)
        for copy in [*xcopies.values(), *zcopies.values()]:
            copy.wait_send()

    return pl.pallas_call(
        body,
        in_specs=[pl.BlockSpec(memory_space=pltpu.VMEM)],
        out_specs=pl.BlockSpec(memory_space=pltpu.VMEM),
        out_shape=jax.ShapeDtypeStruct((height, width), F32),
        scratch_shapes=[
            pltpu.VMEM((fast - 1, slows, height, width), BF16),
            pltpu.VMEM((slows - 1, height, width), BF16),
            pltpu.VMEM((slows - 1, height, width), BF16),
            *both(slows * slices * (fast - 1)),
            *both((slows - 1) * slices),
        ],
        compiler_params=talking(call_id),
    )(parts)


def gather(blocks, axis, size, fast, slices, call_id):
    height, width = blocks[0].shape
    slows = size // fast
    step = height // slices
    count = len(blocks)

    def body(*refs):
        ins, outs = refs[:count], refs[count : 2 * count]
        local, *sems = refs[2 * count :]
        xsems, zsems = sems[:2], sems[2:]
        me, slow, quick, _ = grid_of(axis, fast, size)
        greet(axis, slow, quick, slows, fast)
        order = [(k, s) for k in range(count) for s in range(slices)]
        copies, zcopies = [], {}

        def across(k, s, d, src, slot):
            cut = pl.ds(s * step, step)
            for e in range(1, fast):
                b = lax.rem(quick + e, fast)
                where = ((k * slices + s) * slows + d) * (fast - 1) + e - 1
                copies.append(
                    send(src, outs[k].at[slot, cut], xsems, where, axis, slow * fast + b)
                )

        keep = []
        for k, s in order:
            cut = pl.ds(s * step, step)
            for d in range(1, slows):
                there = lax.rem(slow + d, slows) * fast + quick
                zcopies[k, s, d] = send(
                    ins[k].at[cut],
                    outs[k].at[me, cut],
                    zsems,
                    (k * slices + s) * (slows - 1) + d - 1,
                    axis,
                    there,
                )
            across(k, s, 0, ins[k].at[cut], me)
        for k in range(count):
            keep.append(pltpu.make_async_copy(ins[k], outs[k].at[me], local.at[k]))
            keep[-1].start()
        for k, s in order:
            cut = pl.ds(s * step, step)
            for d in range(1, slows):
                slot = lax.rem(slow + slows - d, slows) * fast + quick
                zcopies[k, s, d].wait_recv()
                across(k, s, d, outs[k].at[slot, cut], slot)
        for copy in copies:
            copy.wait()
        for copy in zcopies.values():
            copy.wait_send()
        for copy in keep:
            copy.wait()

    got = pl.pallas_call(
        body,
        in_specs=[pl.BlockSpec(memory_space=pltpu.VMEM)] * count,
        out_specs=[pl.BlockSpec(memory_space=pl.ANY)] * count,
        out_shape=[jax.ShapeDtypeStruct((size, height, width), block.dtype) for block in blocks],
        scratch_shapes=[
            pltpu.SemaphoreType.DMA((count,)),
            *both(count * slices * slows * (fast - 1)),
            *both(count * slices * (slows - 1)),
        ],
        compiler_params=talking(call_id),
    )(*blocks)
    return [whole.reshape(size * height, width) for whole in got]


def total_over(part, axis, size, fast, call_id):
    height, width = part.shape
    slows = size // fast

    def body(p_ref, o_ref, xbuf, ysum, zbuf, *sems):
        xsems, zsems = sems[:2], sems[2:]
        _, slow, quick, _ = grid_of(axis, fast, size)
        greet(axis, slow, quick, slows, fast)
        copies = []
        for e in range(1, fast):
            b = lax.rem(quick + e, fast)
            copies.append(send(p_ref, xbuf.at[quick], xsems, e - 1, axis, slow * fast + b))
        xbuf[quick] = p_ref[...]
        for copy in copies:
            copy.wait()
        total = xbuf[0]
        for b in range(1, fast):
            total += xbuf[b]
        ysum[...] = total
        copies = []
        for d in range(1, slows):
            there = lax.rem(slow + d, slows) * fast + quick
            copies.append(send(ysum, zbuf.at[slow], zsems, d - 1, axis, there))
        zbuf[slow] = total
        for copy in copies:
            copy.wait()
        total = zbuf[0]
        for a in range(1, slows):
            total += zbuf[a]
        o_ref[...] = total

    return pl.pallas_call(
        body,
        in_specs=[pl.BlockSpec(memory_space=pltpu.VMEM)],
        out_specs=pl.BlockSpec(memory_space=pltpu.VMEM),
        out_shape=jax.ShapeDtypeStruct((height, width), F32),
        scratch_shapes=[
            pltpu.VMEM((fast, height, width), F32),
            pltpu.VMEM((height, width), F32),
            pltpu.VMEM((slows, height, width), F32),
            *both(fast - 1),
            *both(slows - 1),
        ],
        compiler_params=talking(call_id),
    )(part)


def labels_all(labels, cols):
    return lax.all_gather(labels, "col", tiled=True)


def shards(
    rows, cols, tokens, gate_weight, up_weight, down_weight, gate_mask, up_mask, down_mask, head_weight, labels
):
    width = gate_weight.shape[1]
    gate_mask = widened(gate_mask, width)
    up_mask = widened(up_mask, width)
    down_mask = widened(down_mask, down_weight.shape[1])
    near = rows // 4
    mine = tokens.shape[0]
    (every_token,) = gather([tokens], "col", cols, 2, 2, 1)
    fold_part = head_part(down_weight, down_mask, head_weight)
    token_part = dot(every_token, head_weight, 1, 0).astype(BF16)
    classes = head_weight.shape[1]
    piece = width // rows
    both_parts = jnp.concatenate(
        [fold_part.reshape(rows, piece, classes), token_part.reshape(rows, -1, classes)], axis=1
    )
    both_sums = reduce_scatter(both_parts, "row", near, 1, 4)
    (fold,) = gather([both_sums[:piece].astype(BF16)], "row", rows, near, 1, 5)
    parts = gate_up_parts(every_token, gate_weight, up_weight, gate_mask, up_mask, rows)
    share = parts.shape[2]
    stacked = reduce_scatter(parts.reshape(rows, 2 * share, width), "row", near, 4, 2)
    (sums,) = gather([stacked.astype(BF16)], "row", rows, near, 4, 3)
    gate_sum, up_sum = stacked[:share], stacked[share:]
    hidden = (gate_sum * jax.nn.sigmoid(gate_sum) * up_sum).astype(BF16)
    logits = total_over(dot(hidden, fold, 1, 0), "col", cols, 2, 6) + both_sums[piece:]
    (logits_all,) = gather([logits], "row", rows, near, 1, 7)
    losses, grad_full = classify(logits_all, labels_all(labels, cols))
    token_loss = lax.dynamic_slice_in_dim(losses, lax.axis_index("col") * mine, mine)
    gate_grad, up_grad, down_grad, input_part, dmixed = backward(
        every_token,
        sums.reshape(rows, 2, share, width),
        grad_full.astype(BF16),
        fold,
        head_weight,
        gate_weight,
        up_weight,
        gate_mask,
        up_mask,
        down_mask,
    )
    input_sum = reduce_scatter(input_part.reshape(cols, mine, -1), "col", 2, 2, 8)
    own = lax.dynamic_slice_in_dim(dmixed, lax.axis_index("col") * mine, mine)
    tokens_grad = (own.astype(F32) + input_sum).astype(BF16)
    return (token_loss, tokens_grad, gate_grad, up_grad, down_grad)


def solution(mesh):
    placed = (
        P("col", "row"),
        P("row", "col"),
        P("row", "col"),
        P("col", "row"),
        P("row", "col"),
        P("row", "col"),
        P("col", "row"),
        P("row", None),
        P("col"),
    )
    return jax.shard_map(
        functools.partial(shards, mesh.shape["row"], mesh.shape["col"]),
        mesh=mesh,
        in_specs=placed,
        out_specs=(P("col"), P("col", "row"), P("row", "col"), P("row", "col"), P("col", "row")),
        check_vma=False,
    )
```

```python
import functools

import jax
import jax.numpy as jnp
from jax import lax
from jax.experimental import pallas as pl
from jax.experimental.pallas import tpu as pltpu
from jax.sharding import PartitionSpec as P

loss_scale = 8.0
F32 = jnp.float32
BF16 = jnp.bfloat16
MESH = pl.DeviceIdType.MESH


def tile_of(width):
    for tile in (512, 256, 128):
        if width % tile == 0:
            return tile
    return width


def widened(mask, width):
    return jnp.repeat(mask.astype(F32), width // mask.shape[1], axis=1)


def pruned(values, mask):
    height, breadth = values.shape
    blocks = mask.shape[0]
    split = values.reshape(blocks, height // blocks, breadth)
    kept = split * mask[:, None, :].astype(values.dtype)
    return kept.reshape(height, breadth)


def dot(a, b, a_axis, b_axis):
    return lax.dot_general(a, b, (((a_axis,), (b_axis,)), ((), ())), preferred_element_type=F32)


def run(body, grid, in_specs, out_specs, out_shape, flops, touched, scratch=()):
    return pl.pallas_call(
        body,
        grid=grid,
        in_specs=in_specs,
        out_specs=out_specs,
        out_shape=out_shape,
        scratch_shapes=list(scratch),
        compiler_params=pltpu.CompilerParams(vmem_limit_bytes=40 << 20),
        cost_estimate=pl.CostEstimate(flops=flops, bytes_accessed=touched, transcendentals=0),
    )


def head_part(down, mask, head):
    width, depth = down.shape
    classes = head.shape[1]
    tile = tile_of(width)
    steps = width // tile
    mask = mask.reshape(steps, -1, depth)

    def body(w_ref, m_ref, h_ref, o_ref):
        o_ref[...] = dot(pruned(w_ref[...], m_ref[0]), h_ref[...], 1, 0).astype(BF16)

    return run(
        body,
        (steps,),
        [
            pl.BlockSpec((tile, depth), lambda j: (j, 0)),
            pl.BlockSpec((1, mask.shape[1], depth), lambda j: (j, 0, 0)),
            pl.BlockSpec((depth, classes), lambda j: (0, 0)),
        ],
        pl.BlockSpec((tile, classes), lambda j: (j, 0)),
        jax.ShapeDtypeStruct((width, classes), BF16),
        2 * classes * depth * width,
        2 * depth * width,
    )(down, mask, head)


def backward(x, sums, dlogits, fold, head, gate, up, gate_mask, up_mask, down_mask):
    _, steps, owners, share, tile = sums.shape
    tokens, depth = x.shape
    width = gate.shape[1]
    classes = dlogits.shape[1]
    blocks = gate_mask.shape[0]
    down_mask = down_mask.reshape(steps, -1, depth)

    def body(x_ref, s_ref, d_ref, f_ref, h_ref, g_ref, u_ref, gm_ref, um_ref, dm_ref, gg_ref, ug_ref, dg_ref, o_ref, mix_ref, acc, dmixed):
        j = pl.program_id(0)

        @pl.when(j == 0)
        def _():
            dmixed[...] = dot(d_ref[...], h_ref[...], 1, 1).astype(BF16)
            mix_ref[...] = dmixed[...]

        dhidden = dot(d_ref[...], f_ref[...], 1, 1)
        gate_sum = s_ref[0, 0].reshape(tokens, tile).astype(F32)
        up_sum = s_ref[1, 0].reshape(tokens, tile).astype(F32)
        sigmoid_gate = jax.nn.sigmoid(gate_sum)
        activated = gate_sum * sigmoid_gate
        hidden = (activated * up_sum).astype(BF16)
        gate_delta = (dhidden * up_sum * sigmoid_gate * (1.0 + gate_sum * (1.0 - sigmoid_gate))).astype(BF16)
        up_delta = (dhidden * activated).astype(BF16)
        gg_ref[...] = pruned(dot(x_ref[...], gate_delta, 0, 0), gm_ref[...]).astype(BF16)
        ug_ref[...] = pruned(dot(x_ref[...], up_delta, 0, 0), um_ref[...]).astype(BF16)
        dg_ref[...] = pruned(dot(hidden, dmixed[...], 0, 0), dm_ref[0]).astype(BF16)
        part = dot(gate_delta, pruned(g_ref[...], gm_ref[...]), 1, 1)
        part += dot(up_delta, pruned(u_ref[...], um_ref[...]), 1, 1)

        @pl.when(j == 0)
        def _():
            acc[...] = part

        @pl.when(j > 0)
        def _():
            acc[...] += part

        @pl.when(j == steps - 1)
        def _():
            o_ref[...] = acc[...].astype(BF16)

    weight = pl.BlockSpec((depth, tile), lambda j: (0, j))
    mask = pl.BlockSpec((blocks, tile), lambda j: (0, j))
    whole = lambda *shape: pl.BlockSpec(shape, lambda j: (0,) * len(shape))
    return run(
        body,
        (steps,),
        [
            whole(tokens, depth),
            pl.BlockSpec((2, 1, owners, share, tile), lambda j: (0, j, 0, 0, 0)),
            whole(tokens, classes),
            pl.BlockSpec((tile, classes), lambda j: (j, 0)),
            whole(depth, classes),
            weight,
            weight,
            mask,
            mask,
            pl.BlockSpec((1, down_mask.shape[1], depth), lambda j: (j, 0, 0)),
        ],
        [weight, weight, pl.BlockSpec((tile, depth), lambda j: (j, 0)), whole(tokens, depth), whole(tokens, depth)],
        [
            jax.ShapeDtypeStruct((depth, width), BF16),
            jax.ShapeDtypeStruct((depth, width), BF16),
            jax.ShapeDtypeStruct((width, depth), BF16),
            jax.ShapeDtypeStruct((tokens, depth), BF16),
            jax.ShapeDtypeStruct((tokens, depth), BF16),
        ],
        10 * tokens * depth * width,
        10 * depth * width,
        [pltpu.VMEM((tokens, depth), F32), pltpu.VMEM((tokens, depth), BF16)],
    )(x, sums, dlogits, fold, head, gate, up, gate_mask, up_mask, down_mask)


def grid_of(axis, fast, size):
    me = lax.axis_index(axis)
    return me, lax.div(me, fast), lax.rem(me, fast), size // fast


def greet(axis, slow, quick, slows, fast):
    barrier = pltpu.get_barrier_semaphore()
    for d in range(1, fast):
        there = slow * fast + lax.rem(quick + d, fast)
        pl.semaphore_signal(barrier, inc=1, device_id={axis: there}, device_id_type=MESH)
    for d in range(1, slows):
        there = lax.rem(slow + d, slows) * fast + quick
        pl.semaphore_signal(barrier, inc=1, device_id={axis: there}, device_id_type=MESH)
    pl.semaphore_wait(barrier, fast + slows - 2)


def send(src, dst, sems, where, axis, there):
    copy = pltpu.make_async_remote_copy(
        src_ref=src,
        dst_ref=dst,
        send_sem=sems[0].at[where],
        recv_sem=sems[1].at[where],
        device_id={axis: there},
        device_id_type=MESH,
    )
    copy.start()
    return copy


def talking(call_id):
    return pltpu.CompilerParams(
        collective_id=call_id, has_side_effects=True, vmem_limit_bytes=58 << 20
    )


def both(*dims):
    return [pltpu.SemaphoreType.DMA(dims), pltpu.SemaphoreType.DMA(dims)]


def reduce_scatter(parts, axis, fast, slices, call_id):
    size, height, width = parts.shape
    slows = size // fast
    step = height // slices
    group = 16

    def body(p_ref, o_ref, xbuf, ybuf, zbuf, *sems):
        xsems, zsems = sems[:2], sems[2:]
        _, slow, quick, _ = grid_of(axis, fast, size)
        greet(axis, slow, quick, slows, fast)
        order = [(d, s) for s in range(slices) for d in [*range(1, slows), 0]]
        xcopies, zcopies = {}, {}
        for d, s in order:
            a = lax.rem(slow + d, slows)
            cut = pl.ds(s * step, step)
            for e in range(1, fast):
                b = lax.rem(quick + e, fast)
                xcopies[d, s, e] = send(
                    p_ref.at[a * fast + b, cut],
                    xbuf.at[e - 1, d, cut],
                    xsems,
                    (d * slices + s) * (fast - 1) + e - 1,
                    axis,
                    slow * fast + b,
                )
        for d, s in order:
            a = lax.rem(slow + d, slows)
            for e in range(1, fast):
                xcopies[d, s, e].wait_recv()

            def add(i, carry, d=d, s=s, a=a):
                at = pl.ds(pl.multiple_of(s * step + i * group, group), group)
                total = p_ref[a * fast + quick, at].astype(F32)
                for e in range(1, fast):
                    total += xbuf[e - 1, d, at].astype(F32)
                if d == 0:
                    o_ref[at] = total
                else:
                    ybuf[d - 1, at] = total.astype(BF16)
                return carry

            lax.fori_loop(0, step // group, add, 0)
            if d:
                cut = pl.ds(s * step, step)
                zcopies[d, s] = send(
                    ybuf.at[d - 1, cut],
                    zbuf.at[d - 1, cut],
                    zsems,
                    (d - 1) * slices + s,
                    axis,
                    a * fast + quick,
                )
        for s in range(slices):
            for d in range(1, slows):
                zcopies[d, s].wait_recv()

            def close(i, carry, s=s):
                at = pl.ds(pl.multiple_of(s * step + i * group, group), group)
                total = o_ref[at]
                for d in range(1, slows):
                    total += zbuf[d - 1, at].astype(F32)
                o_ref[at] = total
                return carry

            lax.fori_loop(0, step // group, close, 0)
        for copy in [*xcopies.values(), *zcopies.values()]:
            copy.wait_send()

    return pl.pallas_call(
        body,
        in_specs=[pl.BlockSpec(memory_space=pltpu.VMEM)],
        out_specs=pl.BlockSpec(memory_space=pltpu.VMEM),
        out_shape=jax.ShapeDtypeStruct((height, width), F32),
        scratch_shapes=[
            pltpu.VMEM((fast - 1, slows, height, width), BF16),
            pltpu.VMEM((slows - 1, height, width), BF16),
            pltpu.VMEM((slows - 1, height, width), BF16),
            *both(slows * slices * (fast - 1)),
            *both((slows - 1) * slices),
        ],
        compiler_params=talking(call_id),
    )(parts)


def gather(blocks, axis, size, fast, slices, call_id):
    height = blocks[0].shape[0]
    slows = size // fast
    step = height // slices
    count = len(blocks)

    def body(*refs):
        ins, outs = refs[:count], refs[count : 2 * count]
        local, *sems = refs[2 * count :]
        xsems, zsems = sems[:2], sems[2:]
        me, slow, quick, _ = grid_of(axis, fast, size)
        greet(axis, slow, quick, slows, fast)
        order = [(k, s) for k in range(count) for s in range(slices)]
        copies, zcopies = [], {}

        def across(k, s, d, src, slot):
            cut = pl.ds(s * step, step)
            for e in range(1, fast):
                b = lax.rem(quick + e, fast)
                where = ((k * slices + s) * slows + d) * (fast - 1) + e - 1
                copies.append(
                    send(src, outs[k].at[slot, cut], xsems, where, axis, slow * fast + b)
                )

        keep = []
        for k, s in order:
            cut = pl.ds(s * step, step)
            for d in range(1, slows):
                there = lax.rem(slow + d, slows) * fast + quick
                zcopies[k, s, d] = send(
                    ins[k].at[cut],
                    outs[k].at[me, cut],
                    zsems,
                    (k * slices + s) * (slows - 1) + d - 1,
                    axis,
                    there,
                )
            across(k, s, 0, ins[k].at[cut], me)
        for k in range(count):
            keep.append(pltpu.make_async_copy(ins[k], outs[k].at[me], local.at[k]))
            keep[-1].start()
        for k, s in order:
            cut = pl.ds(s * step, step)
            for d in range(1, slows):
                slot = lax.rem(slow + slows - d, slows) * fast + quick
                zcopies[k, s, d].wait_recv()
                across(k, s, d, outs[k].at[slot, cut], slot)
        for copy in copies:
            copy.wait()
        for copy in zcopies.values():
            copy.wait_send()
        for copy in keep:
            copy.wait()

    got = pl.pallas_call(
        body,
        in_specs=[pl.BlockSpec(memory_space=pltpu.VMEM)] * count,
        out_specs=[pl.BlockSpec(memory_space=pl.ANY)] * count,
        out_shape=[jax.ShapeDtypeStruct((size, *block.shape), block.dtype) for block in blocks],
        scratch_shapes=[
            pltpu.SemaphoreType.DMA((count,)),
            *both(count * slices * slows * (fast - 1)),
            *both(count * slices * (slows - 1)),
        ],
        compiler_params=talking(call_id),
    )(*blocks)
    return [whole.reshape(-1, whole.shape[2]) for whole in got]


ENDS = 2


def place(rows):
    fast = rows // 4
    me, z, x, slows = grid_of("row", fast, rows)
    return me, z, x, fast, slows


def chain(end, z, slows):
    if end:
        return slows - 1 - z, 1, z == slows - 1, z == 0
    return z, -1, z == 0, z == slows - 1


def owner_row(block, fast, slows):
    return jnp.where(block < fast, block, block + (slows - 2) * fast)


def greet_rows(rows, cols=None):
    barrier = pltpu.get_barrier_semaphore()
    me = lax.axis_index("row")
    for d in range(1, rows):
        pl.semaphore_signal(barrier, inc=1, device_id={"row": lax.rem(me + d, rows)}, device_id_type=MESH)
    total = rows - 1
    if cols is not None:
        mine = lax.axis_index("col")
        for d in range(1, cols):
            pl.semaphore_signal(barrier, inc=1, device_id={"col": lax.rem(mine + d, cols)}, device_id_type=MESH)
        total += cols - 1
    pl.semaphore_wait(barrier, total)


def to(src, dst, sems, at, **there):
    return pltpu.make_async_remote_copy(
        src_ref=src,
        dst_ref=dst,
        send_sem=sems[0].at[at],
        recv_sem=sems[1].at[at],
        device_id=there,
        device_id_type=MESH,
    )


def by_rows(count, step, work):
    def go(i, carry):
        work(pl.ds(pl.multiple_of(i * step, step), step))
        return carry

    lax.fori_loop(0, count // step, go, 0)


def width_of_step(width):
    return 256 if width % 256 == 0 else 128


def forward(x_all, gate, up, gate_mask, up_mask, fold, token_logits, rows, call_id):
    tokens, depth = x_all.shape
    width = gate.shape[1]
    classes = fold.shape[1]
    fast, slows = rows // 4, 4
    owners = ENDS * fast
    share = tokens // owners
    step = width_of_step(width)
    tiles = width // step
    blocks = gate_mask.shape[0]
    group = 32

    def body(x_ref, g_hbm, u_hbm, gm_ref, um_ref, f_ref, t_ref, sums_ref, logit_ref, weights, parts, xa, za, zb, xb, gates, tbuf, *sems):
        xa_sems, za_sems, zb_sems, xb_sems, t_sems, w_sems = sems[:2], sems[2:4], sems[4:6], sems[6:8], sems[8:10], sems[10]
        me, z, x, _, _ = place(rows)

        def fetch(t, k):
            cut = pl.ds(pl.multiple_of(t * step, step), step)
            return pltpu.make_async_copy((g_hbm, u_hbm)[k].at[:, cut], weights.at[k, t], w_sems.at[k, t])

        def start_fetch(t, carry):
            for k in range(2):
                fetch(t, k).start()
            return carry

        lax.fori_loop(0, tiles, start_fetch, 0)
        greet_rows(rows)

        def cross(t, end, e):
            there = lax.rem(x + e, fast)
            return to(parts.at[0, t, end * fast + there], xa.at[t, end, e - 1], xa_sems, (t, end, e - 1), row=z * fast + there)

        def gate_hop(t, end, towards):
            return to(parts.at[0, t, end * fast + x], za.at[t, end], za_sems, (t, end), row=(z + towards) * fast + x)

        def up_hop(t, end, towards):
            return to(parts.at[1, t, pl.ds(end * fast, fast)], zb.at[t, end], zb_sems, (t, end), row=(z + towards) * fast + x)

        def up_cross(t, end, e):
            there = lax.rem(x + e, fast)
            return to(parts.at[1, t, end * fast + there], xb.at[t, e - 1], xb_sems, (t, e - 1), row=z * fast + there)

        block = lax.axis_index("col")
        home = owner_row(block, fast, slows)
        away = lax.rem(me - home + rows, rows)

        def token_copy(slot):
            return to(t_ref, tbuf.at[slot], t_sems, slot, row=home)

        @pl.when(me != home)
        def _():
            token_copy(away - 1).start()

        logit_ref[...] = jnp.zeros_like(logit_ref)

        def slot(s, carry):
            @pl.when(s < tiles)
            def _():
                t = s
                for k, m in enumerate((gm_ref, um_ref)):
                    fetch(t, k).wait()
                    part = dot(x_ref[...], pruned(weights[k, t], m[t]), 1, 0).astype(BF16)
                    parts[k, t] = part.reshape(owners, share, step)
                    for end in range(ENDS):
                        if k == 0:
                            for e in range(1, fast):
                                cross(t, end, e).start()
                        else:
                            _, towards, _, far = chain(end, z, slows)

                            @pl.when(far)
                            def _(end=end, towards=towards):
                                up_hop(t, end, towards).start()

            for end in range(ENDS):
                hops, towards, own, far = chain(end, z, slows)
                t = s - 1 - (slows - 1 - hops)
                inside = jnp.logical_and(t >= 0, t < tiles)

                @pl.when(inside)
                def _(end=end, t=t, towards=towards, own=own, far=far):
                    at = end * fast + x
                    for e in range(1, fast):
                        cross(t, end, e).wait_recv()

                    @pl.when(far)
                    def _():
                        def add(cut):
                            total = parts[0, t, at, cut].astype(F32)
                            for e in range(1, fast):
                                total += xa[t, end, e - 1, cut].astype(F32)
                            parts[0, t, at, cut] = total.astype(BF16)

                        by_rows(share, group, add)

                    @pl.when(jnp.logical_not(far))
                    def _():
                        gate_hop(t, end, towards).wait_recv()

                        def add(cut):
                            total = parts[0, t, at, cut].astype(F32) + za[t, end, cut].astype(F32)
                            for e in range(1, fast):
                                total += xa[t, end, e - 1, cut].astype(F32)
                            parts[0, t, at, cut] = total.astype(BF16)

                            @pl.when(own)
                            def _():
                                gates[t, cut] = total

                        by_rows(share, group, add)

                    @pl.when(jnp.logical_not(own))
                    def _():
                        gate_hop(t, end, towards).start()

                    @pl.when(jnp.logical_not(far))
                    def _():
                        up_hop(t, end, towards).wait_recv()

                        def add_block(b):
                            def add(cut):
                                total = parts[1, t, end * fast + b, cut].astype(F32) + zb[t, end, b, cut].astype(F32)
                                parts[1, t, end * fast + b, cut] = total.astype(BF16)

                            by_rows(share, group, add)

                        @pl.when(jnp.logical_not(own))
                        def _():
                            for b in range(fast):
                                add_block(b)
                            up_hop(t, end, towards).start()

                        @pl.when(own)
                        def _():
                            for e in range(1, fast):
                                add_block(lax.rem(x + e, fast))
                                up_cross(t, end, e).start()

            for end in range(ENDS):
                _, _, own, _ = chain(end, z, slows)
                t = s - 1 - slows
                done = jnp.logical_and(own, jnp.logical_and(t >= 0, t < tiles))

                @pl.when(done)
                def _(end=end, t=t):
                    for e in range(1, fast):
                        up_cross(t, end, e).wait_recv()

                    def close(cut):
                        up_sum = parts[1, t, end * fast + x, cut].astype(F32) + zb[t, end, x, cut].astype(F32)
                        for e in range(1, fast):
                            up_sum += xb[t, e - 1, cut].astype(F32)
                        gate_sum = gates[t, cut]
                        sums_ref[0, t, cut] = gate_sum.astype(BF16)
                        sums_ref[1, t, cut] = up_sum.astype(BF16)
                        hidden = (gate_sum * jax.nn.sigmoid(gate_sum) * up_sum).astype(BF16)
                        logit_ref[cut] += dot(hidden, f_ref[t], 1, 0)

                    by_rows(share, share, close)

            return carry

        lax.fori_loop(0, tiles + slows + 1, slot, 0)

        @pl.when(me == home)
        def _():
            for d in range(1, rows):
                token_copy(d - 1).wait_recv()
            total = t_ref[...]
            for d in range(1, rows):
                total += tbuf[d - 1]
            logit_ref[...] += total

        @pl.when(me != home)
        def _():
            token_copy(away - 1).wait_send()

        def drain(t, carry):
            for end in range(ENDS):
                _, towards, own, far = chain(end, z, slows)
                for e in range(1, fast):
                    cross(t, end, e).wait_send()

                @pl.when(jnp.logical_not(own))
                def _(end=end, towards=towards):
                    gate_hop(t, end, towards).wait_send()
                    up_hop(t, end, towards).wait_send()

                @pl.when(own)
                def _(end=end):
                    for e in range(1, fast):
                        up_cross(t, end, e).wait_send()

            return carry

        lax.fori_loop(0, tiles, drain, 0)

    vmem = pl.BlockSpec(memory_space=pltpu.VMEM)
    hbm = pl.BlockSpec(memory_space=pl.ANY)
    masks = [m.reshape(blocks, tiles, step).transpose(1, 0, 2) for m in (gate_mask, up_mask)]
    return pl.pallas_call(
        body,
        in_specs=[vmem, hbm, hbm, vmem, vmem, vmem, vmem],
        out_specs=[vmem, vmem],
        out_shape=[
            jax.ShapeDtypeStruct((2, tiles, share, step), BF16),
            jax.ShapeDtypeStruct((share, classes), F32),
        ],
        scratch_shapes=[
            pltpu.VMEM((2, tiles, depth, step), BF16),
            pltpu.VMEM((2, tiles, owners, share, step), BF16),
            pltpu.VMEM((tiles, ENDS, fast - 1, share, step), BF16),
            pltpu.VMEM((tiles, ENDS, share, step), BF16),
            pltpu.VMEM((tiles, ENDS, fast, share, step), BF16),
            pltpu.VMEM((tiles, fast - 1, share, step), BF16),
            pltpu.VMEM((tiles, share, step), F32),
            pltpu.VMEM((rows - 1, share, classes), F32),
            *both(tiles, ENDS, fast - 1),
            *both(tiles, ENDS),
            *both(tiles, ENDS),
            *both(tiles, fast - 1),
            *both(rows - 1),
            pltpu.SemaphoreType.DMA((2, tiles)),
        ],
        compiler_params=talking(call_id),
    )(x_all, gate, up, *masks, fold.reshape(tiles, step, classes), token_logits)


def spread(sums, partial, onehot, rows, cols, call_id):
    _, tiles, share, step = sums.shape
    classes = partial.shape[1]
    fast, slows = rows // 4, 4
    owners = ENDS * fast

    def body(s_ref, p_ref, h_ref, all_ref, grads, loss_ref, lbuf, *sems):
        za_sems, xa_sems, zb_sems, xb_sems, l_sems, d_sems, loss_sems, local = (
            sems[:2], sems[2:4], sems[4:6], sems[6:8], sems[8:10], sems[10:12], sems[12:14], sems[14]
        )
        me, z, x, _, _ = place(rows)
        col = lax.axis_index("col")
        greet_rows(rows, cols)
        mine = jnp.where(z == 0, x, fast + x)
        owning = jnp.logical_or(z == 0, z == slows - 1)

        def gate_hop(t, end, towards):
            q = end * fast + x
            return to(all_ref.at[0, t, q], all_ref.at[0, t, q], za_sems, (t, end), row=(z - towards) * fast + x)

        def gate_cross(t, end, e):
            q = end * fast + x
            return to(all_ref.at[0, t, q], all_ref.at[0, t, q], xa_sems, (t, end, e - 1), row=z * fast + lax.rem(x + e, fast))

        def gate_got(t, end, e):
            q = end * fast + lax.rem(x + fast - e, fast)
            return to(all_ref.at[0, t, q], all_ref.at[0, t, q], xa_sems, (t, end, e - 1), row=z * fast + lax.rem(x + e, fast))

        def up_hop(t, end, towards):
            cut = pl.ds(end * fast, fast)
            return to(all_ref.at[1, t, cut], all_ref.at[1, t, cut], zb_sems, (t, end), row=(z - towards) * fast + x)

        def up_cross(t, end, e):
            q = end * fast + x
            return to(all_ref.at[1, t, q], all_ref.at[1, t, q], xb_sems, (t, e - 1), row=z * fast + lax.rem(x + e, fast))

        def up_got(t, end, e):
            q = end * fast + lax.rem(x + fast - e, fast)
            return to(all_ref.at[1, t, q], all_ref.at[1, t, q], xb_sems, (t, e - 1), row=z * fast + lax.rem(x + e, fast))

        def keep(t, k):
            return pltpu.make_async_copy(s_ref.at[k, t], all_ref.at[k, t, mine], local.at[k, t])

        def logit_copy(d):
            return to(p_ref, lbuf.at[col], l_sems, d - 1, col=lax.rem(col + d, cols))

        def logit_got(d):
            return to(p_ref, lbuf.at[lax.rem(col + cols - d, cols)], l_sems, d - 1, col=lax.rem(col + d, cols))

        def grad_copy(d):
            there = lax.rem(me + d, rows)
            return pltpu.make_async_remote_copy(
                src_ref=grads.at[mine],
                dst_ref=grads.at[mine],
                send_sem=d_sems[0].at[d - 1],
                recv_sem=d_sems[1].at[mine],
                device_id={"row": there},
                device_id_type=MESH,
            )

        def grad_got(q):
            return pltpu.make_async_remote_copy(
                src_ref=grads.at[q],
                dst_ref=grads.at[q],
                send_sem=d_sems[0].at[0],
                recv_sem=d_sems[1].at[q],
                device_id={"row": lax.rem(me + 1, rows)},
                device_id_type=MESH,
            )

        def loss_copy(d):
            return pltpu.make_async_remote_copy(
                src_ref=loss_ref,
                dst_ref=loss_ref,
                send_sem=loss_sems[0].at[d - 1],
                recv_sem=loss_sems[1].at[0],
                device_id={"row": lax.rem(me + d, rows)},
                device_id_type=MESH,
            )

        @pl.when(owning)
        def _():
            for d in range(1, cols):
                logit_copy(d).start()
            lbuf[col] = p_ref[...]

            def keeps(t, carry):
                for k in range(2):
                    keep(t, k).start()
                return carry

            lax.fori_loop(0, tiles, keeps, 0)
            for d in range(1, cols):
                logit_got(d).wait_recv()
            logits = lbuf[0]
            for c in range(1, cols):
                logits += lbuf[c]
            onehot_here = h_ref[mine].astype(F32)
            exponent = jnp.exp(logits)
            partition = jnp.sum(exponent, axis=1, keepdims=True)
            grads[mine] = (loss_scale * (exponent / partition - onehot_here)).astype(BF16)
            for d in range(1, rows):
                grad_copy(d).start()

            @pl.when(mine == col)
            def _():
                cost = jnp.log(partition) - jnp.sum(logits * onehot_here, axis=1, keepdims=True)
                loss_ref[...] = jnp.transpose(jnp.broadcast_to(cost, (share, 128)))[:8]
                for d in range(1, rows):
                    loss_copy(d).start()

            def kept(t, carry):
                for k in range(2):
                    keep(t, k).wait()
                return carry

            lax.fori_loop(0, tiles, kept, 0)

        def slot(s, carry):
            for end in range(ENDS):
                hops, towards, own, far = chain(end, z, slows)
                t = s - hops

                @pl.when(jnp.logical_and(t >= 0, t < tiles))
                def _(end=end, t=t, towards=towards, own=own, far=far):
                    @pl.when(jnp.logical_not(own))
                    def _():
                        gate_hop(t, end, towards).wait_recv()

                    @pl.when(jnp.logical_not(far))
                    def _():
                        gate_hop(t, end, towards).start()

                    for e in range(1, fast):
                        gate_cross(t, end, e).start()

                    @pl.when(own)
                    def _():
                        for e in range(1, fast):
                            up_cross(t, end, e).start()

                t = s - hops - 1

                @pl.when(jnp.logical_and(t >= 0, t < tiles))
                def _(end=end, t=t, towards=towards, own=own, far=far):
                    @pl.when(own)
                    def _():
                        for e in range(1, fast):
                            up_got(t, end, e).wait_recv()

                    @pl.when(jnp.logical_not(own))
                    def _():
                        up_hop(t, end, towards).wait_recv()

                    @pl.when(jnp.logical_not(far))
                    def _():
                        up_hop(t, end, towards).start()

            t = s - slows

            @pl.when(t >= 0)
            def _():
                for end in range(ENDS):
                    for e in range(1, fast):
                        gate_got(t, end, e).wait_recv()

            return carry

        lax.fori_loop(0, tiles + slows, slot, 0)

        for q in range(owners):
            home = q if q < fast else q + (slows - 2) * fast

            @pl.when(me != home)
            def _(q=q):
                grad_got(q).wait_recv()

        home = owner_row(col, fast, slows)

        @pl.when(me != home)
        def _():
            loss_copy(1).wait_recv()

        @pl.when(me == home)
        def _():
            for d in range(1, rows):
                loss_copy(d).wait_send()

        @pl.when(owning)
        def _():
            for d in range(1, cols):
                logit_copy(d).wait_send()
            for d in range(1, rows):
                grad_copy(d).wait_send()

        def drain(t, carry):
            for end in range(ENDS):
                _, towards, own, far = chain(end, z, slows)
                for e in range(1, fast):
                    gate_cross(t, end, e).wait_send()

                @pl.when(jnp.logical_not(far))
                def _(end=end, towards=towards):
                    gate_hop(t, end, towards).wait_send()
                    up_hop(t, end, towards).wait_send()

                @pl.when(own)
                def _(end=end):
                    for e in range(1, fast):
                        up_cross(t, end, e).wait_send()

            return carry

        lax.fori_loop(0, tiles, drain, 0)

    vmem = pl.BlockSpec(memory_space=pltpu.VMEM)
    return pl.pallas_call(
        body,
        in_specs=[vmem, vmem, vmem],
        out_specs=[vmem, vmem, vmem],
        out_shape=[
            jax.ShapeDtypeStruct((2, tiles, owners, share, step), BF16),
            jax.ShapeDtypeStruct((owners, share, classes), BF16),
            jax.ShapeDtypeStruct((8, share), F32),
        ],
        scratch_shapes=[
            pltpu.VMEM((cols, share, classes), F32),
            *both(tiles, ENDS),
            *both(tiles, ENDS, fast - 1),
            *both(tiles, ENDS),
            *both(tiles, fast - 1),
            *both(cols - 1),
            pltpu.SemaphoreType.DMA((rows - 1,)),
            pltpu.SemaphoreType.DMA((owners,)),
            pltpu.SemaphoreType.DMA((rows - 1,)),
            pltpu.SemaphoreType.DMA((1,)),
            pltpu.SemaphoreType.DMA((2, tiles)),
        ],
        compiler_params=talking(call_id),
    )(sums, partial, onehot)


def shards(
    rows, cols, tokens, gate_weight, up_weight, down_weight, gate_mask, up_mask, down_mask, head_weight, labels
):
    width = gate_weight.shape[1]
    gate_mask = widened(gate_mask, width)
    up_mask = widened(up_mask, width)
    down_mask = widened(down_mask, down_weight.shape[1])
    near = rows // 4
    mine = tokens.shape[0]
    classes = head_weight.shape[1]
    onehot = (labels[:, None] == lax.broadcasted_iota(jnp.int32, (mine, classes), 1)).astype(BF16)
    every_token, every_onehot = gather([tokens, onehot], "col", cols, 2, 2, 1)
    fold_part = head_part(down_weight, down_mask, head_weight)
    fold_sum = reduce_scatter(fold_part.reshape(rows, width // rows, classes), "row", near, 1, 2)
    (fold,) = gather([fold_sum.astype(BF16)], "row", rows, near, 1, 3)
    sums, partial = forward(
        every_token, gate_weight, up_weight, gate_mask, up_mask, fold, dot(tokens, head_weight, 1, 0), rows, 4
    )
    every_sum, dlogits, losses = spread(
        sums, partial, every_onehot.reshape(-1, sums.shape[2], classes), rows, cols, 5
    )
    token_loss = losses[0]
    gate_grad, up_grad, down_grad, input_part, dmixed = backward(
        every_token,
        every_sum,
        dlogits.reshape(-1, classes),
        fold,
        head_weight,
        gate_weight,
        up_weight,
        gate_mask,
        up_mask,
        down_mask,
    )
    input_sum = reduce_scatter(input_part.reshape(cols, mine, -1), "col", 2, 2, 6)
    own = lax.dynamic_slice_in_dim(dmixed, lax.axis_index("col") * mine, mine)
    tokens_grad = (own.astype(F32) + input_sum).astype(BF16)
    return (token_loss, tokens_grad, gate_grad, up_grad, down_grad)


def solution(mesh):
    placed = (
        P("col", "row"),
        P("row", "col"),
        P("row", "col"),
        P("col", "row"),
        P("row", "col"),
        P("row", "col"),
        P("col", "row"),
        P("row", None),
        P("col"),
    )
    return jax.shard_map(
        functools.partial(shards, mesh.shape["row"], mesh.shape["col"]),
        mesh=mesh,
        in_specs=placed,
        out_specs=(P("col"), P("col", "row"), P("row", "col"), P("row", "col"), P("col", "row")),
        check_vma=False,
    )
```

```python
import functools

import jax
import jax.numpy as jnp
from jax import lax
from jax.experimental import pallas as pl
from jax.experimental.pallas import tpu as pltpu
from jax.sharding import PartitionSpec as P

loss_scale = 8.0
F32 = jnp.float32
BF16 = jnp.bfloat16
MESH = pl.DeviceIdType.MESH


def tile_of(width):
    for tile in (512, 256, 128):
        if width % tile == 0:
            return tile
    return width


def pruned(values, mask):
    height, breadth = values.shape
    blocks = mask.shape[0]
    split = values.reshape(blocks, height // blocks, breadth)
    kept = split * mask[:, None, :].astype(values.dtype)
    return kept.reshape(height, breadth)


def dot(a, b, a_axis, b_axis):
    return lax.dot_general(a, b, (((a_axis,), (b_axis,)), ((), ())), preferred_element_type=F32)


def run(body, grid, in_specs, out_specs, out_shape, flops, touched, scratch=()):
    return pl.pallas_call(
        body,
        grid=grid,
        in_specs=in_specs,
        out_specs=out_specs,
        out_shape=out_shape,
        scratch_shapes=list(scratch),
        compiler_params=pltpu.CompilerParams(vmem_limit_bytes=60 << 20),
        cost_estimate=pl.CostEstimate(flops=flops, bytes_accessed=touched, transcendentals=0),
    )


def weight_grads(turned, deltas, hidden, dmixed, gate_mask, up_mask, down_mask):
    _, tiles, tokens, step = deltas.shape
    depth = turned.shape[0]
    width = tiles * step
    steps = down_mask.shape[0]
    pair = tiles // steps
    span = pair * step
    blocks = gate_mask.shape[1]

    def body(x_ref, d_ref, h_ref, m_ref, gm_ref, um_ref, dm_ref, gg_ref, ug_ref, dg_ref):
        for i in range(pair):
            at = slice(i * step, (i + 1) * step)
            for k, (mask, out) in enumerate(((gm_ref, gg_ref), (um_ref, ug_ref))):
                out[:, at] = pruned(dot(x_ref[...], d_ref[k, i], 1, 0), mask[i]).astype(BF16)
        dg_ref[...] = pruned(dot(h_ref[...].reshape(span, tokens), m_ref[...], 1, 0), dm_ref[0]).astype(BF16)

    weight = pl.BlockSpec((depth, span), lambda j: (0, j))
    mask = pl.BlockSpec((pair, blocks, step), lambda j: (j, 0, 0))
    return run(
        body,
        (steps,),
        [
            pl.BlockSpec((depth, tokens), lambda j: (0, 0)),
            pl.BlockSpec((2, pair, tokens, step), lambda j: (0, j, 0, 0)),
            pl.BlockSpec((pair, step, tokens), lambda j: (j, 0, 0)),
            pl.BlockSpec((tokens, depth), lambda j: (0, 0)),
            mask,
            mask,
            pl.BlockSpec((1, down_mask.shape[1], depth), lambda j: (j, 0, 0)),
        ],
        [weight, weight, pl.BlockSpec((span, depth), lambda j: (j, 0))],
        [
            jax.ShapeDtypeStruct((depth, width), BF16),
            jax.ShapeDtypeStruct((depth, width), BF16),
            jax.ShapeDtypeStruct((width, depth), BF16),
        ],
        6 * tokens * depth * width,
        10 * depth * width,
    )(turned, deltas, hidden, dmixed, gate_mask, up_mask, down_mask)


def grid_of(axis, fast, size):
    me = lax.axis_index(axis)
    return me, lax.div(me, fast), lax.rem(me, fast), size // fast


def talking(call_id):
    return pltpu.CompilerParams(
        collective_id=call_id, has_side_effects=True, vmem_limit_bytes=60 << 20
    )


def both(*dims):
    return [pltpu.SemaphoreType.DMA(dims), pltpu.SemaphoreType.DMA(dims)]


ENDS = 2
LAG = 2
LAG_CROSS = 1


def place(rows):
    fast = rows // 4
    me, z, x, slows = grid_of("row", fast, rows)
    return me, z, x, fast, slows


def chain(end, z, slows):
    if end:
        return slows - 1 - z, 1, z == slows - 1, z == 0
    return z, -1, z == 0, z == slows - 1


def owner_row(block, fast, slows):
    return jnp.where(block < fast, block, block + (slows - 2) * fast)


def greet_rows(rows, cols=None):
    barrier = pltpu.get_barrier_semaphore()
    me = lax.axis_index("row")
    for d in range(1, rows):
        pl.semaphore_signal(barrier, inc=1, device_id={"row": lax.rem(me + d, rows)}, device_id_type=MESH)
    total = rows - 1
    if cols is not None:
        mine = lax.axis_index("col")
        for d in range(1, cols):
            pl.semaphore_signal(barrier, inc=1, device_id={"col": lax.rem(mine + d, cols)}, device_id_type=MESH)
        total += cols - 1
    pl.semaphore_wait(barrier, total)


def to(src, dst, sems, at, **there):
    return pltpu.make_async_remote_copy(
        src_ref=src,
        dst_ref=dst,
        send_sem=sems[0].at[at],
        recv_sem=sems[1].at[at],
        device_id=there,
        device_id_type=MESH,
    )


def by_rows(count, step, work):
    def go(i, carry):
        work(pl.ds(pl.multiple_of(i * step, step), step))
        return carry

    lax.fori_loop(0, count // step, go, 0)


def width_of_step(width):
    return 256 if width % 256 == 0 else 128


def prepare(tokens, labels, down, masks, head, step, rows, cols, call_id):
    mine, depth = tokens.shape
    width, classes = down.shape[0], head.shape[1]
    tile = tile_of(width)
    steps = width // tile
    tiles = width // step
    gate_mask, up_mask, down_mask = masks
    blocks = gate_mask.shape[0]
    down_mask = down_mask.reshape(steps, -1, down_mask.shape[1])
    fast, slows = rows // 4, 4
    pairs, far = 2, cols // 2
    piece = width // rows
    slices = next(n for n in (4, 7, 2, 1) if piece % (16 * n) == 0)
    span = piece // slices
    halves = 2
    half = mine // halves

    def stretch(mask, first, span, out):
        lanes = out // mask.shape[1]
        kind = (mask.shape[1], span)
        source = lax.broadcasted_iota(jnp.int32, kind, 0)
        target = lax.div(first + lax.broadcasted_iota(jnp.int32, kind, 1), lanes)
        pick = (source == target).astype(F32).astype(BF16)
        return dot(mask.astype(F32).astype(BF16), pick, 1, 0)

    def body(
        x_ref, l_ref, w_hbm, gm_ref, um_ref, m_ref, c_ref,
        x_all, h_all, fold, gate_out, up_out, down_out, token_out,
        h_ref, weights, parts, xbuf, ybuf, zbuf, *sems,
    ):
        xs, zs, cx, cz = (sems[2 * i : 2 * i + 2] for i in range(4))
        w_sems, local = sems[8], sems[9]
        me, z, x, _, _ = place(rows)
        col, slow, quick, _ = grid_of("col", pairs, cols)

        def fetch(t):
            cut = pl.ds(pl.multiple_of(t * tile, tile), tile)
            return pltpu.make_async_copy(w_hbm.at[cut], weights.at[t], w_sems.at[t])

        def start_fetch(t, carry):
            fetch(t).start()
            return carry

        lax.fori_loop(0, steps, start_fetch, 0)
        greet_rows(rows, cols)
        started = []

        def go(copy):
            copy.start()
            started.append(copy)
            return copy

        number = jnp.broadcast_to(l_ref[...], (classes, mine))
        turned = (number == lax.broadcasted_iota(jnp.int32, (classes, mine), 0)).astype(F32)
        h_ref[...] = jnp.transpose(turned).astype(BF16)
        ins, outs = (x_ref, h_ref), (x_all, h_all)
        arrivals = {}

        def across(k, s, d, src, block):
            cut = pl.ds(s * half, half)
            return go(
                to(src, outs[k].at[block, cut], cx, ((k * halves + s) * far + d), col=slow * pairs + lax.rem(quick + 1, pairs))
            )

        for s in range(halves):
            for k in range(2):
                cut = pl.ds(s * half, half)
                for d in range(1, far):
                    there = lax.rem(slow + d, far) * pairs + quick
                    arrivals[k, s, d] = go(
                        to(ins[k].at[cut], outs[k].at[col, cut], cz, ((k * halves + s) * (far - 1) + d - 1), col=there)
                    )
                across(k, s, 0, ins[k].at[cut], col)
        keep = [pltpu.make_async_copy(ins[k], outs[k].at[col], local.at[k]) for k in range(2)]
        for copy in keep:
            copy.start()

        def fold_tile(t, carry):
            fetch(t).wait()
            cut = pl.ds(pl.multiple_of(t * tile, tile), tile)
            down_out[t] = stretch(m_ref[t], 0, depth, depth)
            parts[cut] = dot(pruned(weights[t], down_out[t]), c_ref[...], 1, 0).astype(BF16)
            return carry

        lax.fori_loop(0, steps, fold_tile, 0)

        def rows_of(block, s):
            return pl.ds(pl.multiple_of(block * piece + s * span, 16), span)

        order = [(d, s) for s in range(slices) for d in [*range(1, slows), 0]]
        xcopies, zcopies = {}, {}
        for d, s in order:
            a = lax.rem(z + d, slows)
            for e in range(1, fast):
                b = lax.rem(x + e, fast)
                xcopies[d, s, e] = go(
                    to(
                        parts.at[rows_of(a * fast + b, s)],
                        xbuf.at[e - 1, d, pl.ds(s * span, span)],
                        xs,
                        (d * slices + s) * (fast - 1) + e - 1,
                        row=z * fast + b,
                    )
                )

        def widen(t, carry):
            for mask, out in ((gm_ref, gate_out), (um_ref, up_out)):
                out[t] = stretch(mask[...], t * step, step, width)
            return carry

        lax.fori_loop(0, tiles, widen, 0)
        token_out[...] = dot(x_ref[...], c_ref[...], 1, 0)

        for s in range(halves):
            for k in range(2):
                for d in range(1, far):
                    there = lax.rem(slow + far - d, far) * pairs + quick
                    arrivals[k, s, d].wait_recv()
                    across(k, s, d, outs[k].at[there, pl.ds(s * half, half)], there)

        for d, s in order:
            a = lax.rem(z + d, slows)
            for e in range(1, fast):
                xcopies[d, s, e].wait_recv()
            at = pl.ds(s * span, span)
            total = parts[rows_of(a * fast + x, s)].astype(F32)
            for e in range(1, fast):
                total += xbuf[e - 1, d, at].astype(F32)
            if d:
                ybuf[d - 1, at] = total.astype(BF16)
                zcopies[d, s] = go(
                    to(ybuf.at[d - 1, at], zbuf.at[d - 1, at], zs, (d - 1) * slices + s, row=a * fast + x)
                )
            else:
                parts[rows_of(a * fast + x, s)] = total.astype(BF16)

        for s in range(slices):
            at = pl.ds(s * span, span)
            for d in range(1, slows):
                zcopies[d, s].wait_recv()
            total = parts[rows_of(me, s)].astype(F32)
            for d in range(1, slows):
                total += zbuf[d - 1, at].astype(F32)
            fold[at] = total.astype(BF16)
        received = {id(c) for c in [*xcopies.values(), *zcopies.values(), *arrivals.values()]}
        for copy in started:
            copy.wait_send()
            if id(copy) not in received:
                copy.wait_recv()
        for copy in keep:
            copy.wait()

    vmem = pl.BlockSpec(memory_space=pltpu.VMEM)
    got = pl.pallas_call(
        body,
        in_specs=[vmem, vmem, pl.BlockSpec(memory_space=pl.ANY), vmem, vmem, vmem, vmem],
        out_specs=[vmem] * 7,
        out_shape=[
            jax.ShapeDtypeStruct((cols, mine, depth), BF16),
            jax.ShapeDtypeStruct((cols, mine, classes), BF16),
            jax.ShapeDtypeStruct((piece, classes), BF16),
            jax.ShapeDtypeStruct((tiles, blocks, step), F32),
            jax.ShapeDtypeStruct((tiles, blocks, step), F32),
            jax.ShapeDtypeStruct((steps, down_mask.shape[1], depth), F32),
            jax.ShapeDtypeStruct((mine, classes), F32),
        ],
        scratch_shapes=[
            pltpu.VMEM((mine, classes), BF16),
            pltpu.VMEM((steps, tile, depth), BF16),
            pltpu.VMEM((width, classes), BF16),
            pltpu.VMEM((fast - 1, slows, piece, classes), BF16),
            pltpu.VMEM((slows - 1, piece, classes), BF16),
            pltpu.VMEM((slows - 1, piece, classes), BF16),
            *both(slows * slices * (fast - 1)),
            *both((slows - 1) * slices),
            *both(2 * halves * far),
            *both(2 * halves * (far - 1)),
            pltpu.SemaphoreType.DMA((steps,)),
            pltpu.SemaphoreType.DMA((2,)),
        ],
        compiler_params=talking(call_id),
    )(tokens, labels.reshape(1, mine), down, gate_mask, up_mask, down_mask, head)
    return got[0].reshape(-1, depth), got[1].reshape(-1, classes), *got[2:]


def layer(x_all, onehot, gate, up, gate_mask, up_mask, fold_part, token_logits, head, rows, cols, call_id):
    tokens, depth = x_all.shape
    width = gate.shape[1]
    tiles, blocks, step = gate_mask.shape
    piece, classes = fold_part.shape
    fast, slows = rows // 4, 4
    owners = ENDS * fast
    share = tokens // owners
    group = 32
    mine_rows = tokens // cols
    pairs, far_cols = 2, cols // 2
    slices = 2
    span = mine_rows // slices
    hops_all = LAG * (slows - 1)
    reduced = 2 * LAG_CROSS + hops_all
    begin = max(tiles, reduced)
    arrived = begin + hops_all + LAG_CROSS
    summed = tiles + reduced
    ready = summed + 3
    backlog = max(ready - arrived, 0)

    def body(
        x_ref, h_ref, g_hbm, u_hbm, gm_ref, um_ref, p_ref, t_ref, c_ref,
        deltas_hbm, hidden_hbm, turned, dmixed, tg_ref, loss_ref,
        weights, parts, xa, za, zb, xb, gates, tbuf, logit_ref, fold,
        deltas, hidden_ref, all_ref, grads, lbuf, hbuf, acc, cparts, cx, cy, cz, *sems,
    ):
        (
            xa_sems, za_sems, zb_sems, xb_sems, t_sems, fz_sems, fx_sems,
            gza_sems, gxa_sems, gzb_sems, gxb_sems, l_sems, d_sems, loss_sems, cx_sems, cz_sems,
        ) = (sems[2 * i : 2 * i + 2] for i in range(16))
        w_sems, out_sems = sems[32:]
        me, z, x, _, _ = place(rows)
        col = lax.axis_index("col")
        mine = jnp.where(z == 0, x, fast + x)
        owning = jnp.logical_or(z == 0, z == slows - 1)

        def fetch(t, k):
            cut = pl.ds(pl.multiple_of(t * step, step), step)
            return pltpu.make_async_copy((g_hbm, u_hbm)[k].at[:, cut], weights.at[k, t], w_sems.at[k, t])

        def start_fetch(t, carry):
            for k in range(2):
                fetch(t, k).start()
            return carry

        lax.fori_loop(0, tiles, start_fetch, 0)
        greet_rows(rows, cols)

        def fold_rows(t):
            return pl.ds(pl.multiple_of(t * step, step), step)

        def fold_block(row):
            return fold.at[pl.ds(pl.multiple_of(row * piece, 16), piece)]

        def ring(t):
            return lax.rem(t, 2)

        def fold_hop(d):
            return to(p_ref, fold_block(me), fz_sems, d - 1, row=lax.rem(z + d, slows) * fast + x)

        def fold_got(d):
            block = fold_block(lax.rem(z + slows - d, slows) * fast + x)
            return to(block, block, fz_sems, d - 1, row=lax.rem(z + d, slows) * fast + x)

        def fold_cross(d, e):
            block = fold_block(lax.rem(z + slows - d, slows) * fast + x)
            return to(block, block, fx_sems, (d, e - 1), row=z * fast + lax.rem(x + e, fast))

        def fold_crossed(d, e):
            block = fold_block(lax.rem(z + slows - d, slows) * fast + lax.rem(x + fast - e, fast))
            return to(block, block, fx_sems, (d, e - 1), row=z * fast + lax.rem(x + e, fast))

        def gate_sum_cross(t, end, e):
            there = lax.rem(x + e, fast)
            return to(parts.at[0, t, end * fast + there], xa.at[t, end, e - 1], xa_sems, (t, end, e - 1), row=z * fast + there)

        def gate_sum_hop(t, end, towards):
            return to(parts.at[0, t, end * fast + x], za.at[t, end], za_sems, (t, end), row=(z + towards) * fast + x)

        def up_sum_hop(t, end, towards):
            return to(parts.at[1, t, pl.ds(end * fast, fast)], zb.at[t, end], zb_sems, (t, end), row=(z + towards) * fast + x)

        def up_sum_cross(t, end, e):
            there = lax.rem(x + e, fast)
            return to(parts.at[1, t, end * fast + there], xb.at[t, e - 1], xb_sems, (t, e - 1), row=z * fast + there)

        home = owner_row(col, fast, slows)
        away = lax.rem(me - home + rows, rows)

        def token_copy(slot):
            return to(t_ref, tbuf.at[slot], t_sems, slot, row=home)

        @pl.when(me != home)
        def _():
            token_copy(away - 1).start()

        for d in range(1, slows):
            fold_hop(d).start()
        fold[pl.ds(pl.multiple_of(me * piece, 16), piece)] = p_ref[...]
        for e in range(1, fast):
            fold_cross(0, e).start()
        logit_ref[...] = jnp.zeros_like(logit_ref)
        acc[...] = jnp.zeros_like(acc)

        def reduce_slot(s):
            @pl.when(s < tiles)
            def _():
                t = s
                for k, m in enumerate((gm_ref, um_ref)):
                    fetch(t, k).wait()
                    part = dot(x_ref[...], pruned(weights[k, t], m[t]), 1, 0).astype(BF16)
                    parts[k, t] = part.reshape(owners, share, step)
                    for end in range(ENDS):
                        if k == 0:
                            for e in range(1, fast):
                                gate_sum_cross(t, end, e).start()
                        else:
                            _, towards, _, far = chain(end, z, slows)

                            @pl.when(far)
                            def _(end=end, towards=towards):
                                up_sum_hop(t, end, towards).start()

            for end in range(ENDS):
                hops, towards, own, far = chain(end, z, slows)
                t = s - LAG_CROSS - LAG * (slows - 1 - hops)
                inside = jnp.logical_and(t >= 0, t < tiles)

                @pl.when(inside)
                def _(end=end, t=t, towards=towards, own=own, far=far):
                    at = end * fast + x
                    for e in range(1, fast):
                        gate_sum_cross(t, end, e).wait_recv()

                    @pl.when(far)
                    def _():
                        def add(cut):
                            total = parts[0, t, at, cut].astype(F32)
                            for e in range(1, fast):
                                total += xa[t, end, e - 1, cut].astype(F32)
                            parts[0, t, at, cut] = total.astype(BF16)

                        by_rows(share, group, add)

                    @pl.when(jnp.logical_not(far))
                    def _():
                        gate_sum_hop(t, end, towards).wait_recv()

                        def add(cut):
                            total = parts[0, t, at, cut].astype(F32) + za[t, end, cut].astype(F32)
                            for e in range(1, fast):
                                total += xa[t, end, e - 1, cut].astype(F32)
                            parts[0, t, at, cut] = total.astype(BF16)

                            @pl.when(own)
                            def _():
                                gates[t, cut] = total

                        by_rows(share, group, add)

                    @pl.when(jnp.logical_not(own))
                    def _():
                        gate_sum_hop(t, end, towards).start()

                    @pl.when(jnp.logical_not(far))
                    def _():
                        up_sum_hop(t, end, towards).wait_recv()

                        def add_block(b):
                            def add(cut):
                                total = parts[1, t, end * fast + b, cut].astype(F32) + zb[t, end, b, cut].astype(F32)
                                parts[1, t, end * fast + b, cut] = total.astype(BF16)

                            by_rows(share, group, add)

                        @pl.when(jnp.logical_not(own))
                        def _():
                            for b in range(fast):
                                add_block(b)
                            up_sum_hop(t, end, towards).start()

                        @pl.when(own)
                        def _():
                            for e in range(1, fast):
                                add_block(lax.rem(x + e, fast))
                                up_sum_cross(t, end, e).start()

            for end in range(ENDS):
                _, _, own, _ = chain(end, z, slows)
                t = s - 2 * LAG_CROSS - LAG * (slows - 1)
                done = jnp.logical_and(own, jnp.logical_and(t >= 0, t < tiles))

                @pl.when(done)
                def _(end=end, t=t):
                    for e in range(1, fast):
                        up_sum_cross(t, end, e).wait_recv()

                    def close(cut):
                        up_sum = parts[1, t, end * fast + x, cut].astype(F32) + zb[t, end, x, cut].astype(F32)
                        for e in range(1, fast):
                            up_sum += xb[t, e - 1, cut].astype(F32)
                        gate_sum = gates[t, cut]
                        all_ref[0, t, mine, cut] = gate_sum.astype(BF16)
                        all_ref[1, t, mine, cut] = up_sum.astype(BF16)
                        hidden = (gate_sum * jax.nn.sigmoid(gate_sum) * up_sum).astype(BF16)
                        logit_ref[cut] += dot(hidden, fold[fold_rows(t)], 1, 0)

                    by_rows(share, share, close)


        def gate_hop(t, end, towards):
            q = end * fast + x
            return to(all_ref.at[0, t, q], all_ref.at[0, t, q], gza_sems, (t, end), row=(z - towards) * fast + x)

        def gate_cross(t, end, e):
            q = end * fast + x
            return to(all_ref.at[0, t, q], all_ref.at[0, t, q], gxa_sems, (t, end, e - 1), row=z * fast + lax.rem(x + e, fast))

        def gate_got(t, end, e):
            q = end * fast + lax.rem(x + fast - e, fast)
            return to(all_ref.at[0, t, q], all_ref.at[0, t, q], gxa_sems, (t, end, e - 1), row=z * fast + lax.rem(x + e, fast))

        def up_hop(t, end, towards):
            cut = pl.ds(end * fast, fast)
            return to(all_ref.at[1, t, cut], all_ref.at[1, t, cut], gzb_sems, (t, end), row=(z - towards) * fast + x)

        def up_cross(t, end, e):
            q = end * fast + x
            return to(all_ref.at[1, t, q], all_ref.at[1, t, q], gxb_sems, (t, e - 1), row=z * fast + lax.rem(x + e, fast))

        def up_got(t, end, e):
            q = end * fast + lax.rem(x + fast - e, fast)
            return to(all_ref.at[1, t, q], all_ref.at[1, t, q], gxb_sems, (t, e - 1), row=z * fast + lax.rem(x + e, fast))

        def logit_copy(d):
            return to(logit_ref, lbuf.at[col], l_sems, d - 1, col=lax.rem(col + d, cols))

        def logit_got(d):
            return to(logit_ref, lbuf.at[lax.rem(col + cols - d, cols)], l_sems, d - 1, col=lax.rem(col + d, cols))

        def grad_copy(d):
            there = lax.rem(me + d, rows)
            return pltpu.make_async_remote_copy(
                src_ref=grads.at[mine],
                dst_ref=grads.at[mine],
                send_sem=d_sems[0].at[d - 1],
                recv_sem=d_sems[1].at[mine],
                device_id={"row": there},
                device_id_type=MESH,
            )

        def grad_got(q):
            return pltpu.make_async_remote_copy(
                src_ref=grads.at[q],
                dst_ref=grads.at[q],
                send_sem=d_sems[0].at[0],
                recv_sem=d_sems[1].at[q],
                device_id={"row": lax.rem(me + 1, rows)},
                device_id_type=MESH,
            )

        def loss_copy(d):
            return pltpu.make_async_remote_copy(
                src_ref=loss_ref,
                dst_ref=loss_ref,
                send_sem=loss_sems[0].at[d - 1],
                recv_sem=loss_sems[1].at[0],
                device_id={"row": lax.rem(me + d, rows)},
                device_id_type=MESH,
            )

        def gather_slot(s):
            for end in range(ENDS):
                hops, towards, own, far = chain(end, z, slows)
                t = s - LAG * hops

                @pl.when(jnp.logical_and(t >= 0, t < tiles))
                def _(end=end, t=t, towards=towards, own=own, far=far):
                    @pl.when(jnp.logical_not(own))
                    def _():
                        gate_hop(t, end, towards).wait_recv()

                    @pl.when(jnp.logical_not(far))
                    def _():
                        gate_hop(t, end, towards).start()

                    for e in range(1, fast):
                        gate_cross(t, end, e).start()

                    @pl.when(own)
                    def _():
                        for e in range(1, fast):
                            up_cross(t, end, e).start()

                t = s - LAG * hops - LAG_CROSS

                @pl.when(jnp.logical_and(t >= 0, t < tiles))
                def _(end=end, t=t, towards=towards, own=own, far=far):
                    @pl.when(own)
                    def _():
                        for e in range(1, fast):
                            up_got(t, end, e).wait_recv()

                    @pl.when(jnp.logical_not(own))
                    def _():
                        up_hop(t, end, towards).wait_recv()

                    @pl.when(jnp.logical_not(far))
                    def _():
                        up_hop(t, end, towards).start()

        def results(t):
            return (
                pltpu.make_async_copy(deltas.at[ring(t), 0], deltas_hbm.at[0, t], out_sems.at[0, t]),
                pltpu.make_async_copy(deltas.at[ring(t), 1], deltas_hbm.at[1, t], out_sems.at[1, t]),
                pltpu.make_async_copy(hidden_ref.at[ring(t)], hidden_hbm.at[t], out_sems.at[2, t]),
            )

        def consume(t):
            for end in range(ENDS):
                for e in range(1, fast):
                    gate_got(t, end, e).wait_recv()

            @pl.when(t >= 2)
            def _():
                for copy in results(t - 2):
                    copy.wait()

            def delta(q, carry):
                at = pl.ds(pl.multiple_of(q * share, share), share)
                dhidden = dot(grads[q], fold[fold_rows(t)], 1, 1)
                gate_sum = all_ref[0, t, q].astype(F32)
                up_sum = all_ref[1, t, q].astype(F32)
                sigmoid_gate = jax.nn.sigmoid(gate_sum)
                activated = gate_sum * sigmoid_gate
                hbuf[at] = (activated * up_sum).astype(BF16)
                slope = sigmoid_gate * (1.0 + gate_sum * (1.0 - sigmoid_gate))
                deltas[ring(t), 0, at] = (dhidden * up_sum * slope).astype(BF16)
                deltas[ring(t), 1, at] = (dhidden * activated).astype(BF16)
                return carry

            lax.fori_loop(0, owners, delta, 0)
            hidden_ref[ring(t)] = jnp.transpose(hbuf[...])
            for copy in results(t):
                copy.start()
            part = None
            for k, m in enumerate((gm_ref, um_ref)):
                term = dot(deltas[ring(t), k], pruned(weights[k, t], m[t]), 1, 1)
                part = term if part is None else part + term
            acc[...] += part

        def slot(s, carry):
            reduce_slot(s)
            gather_slot(s - begin)
            return carry

        lax.fori_loop(0, 3, slot, 0)
        for d in range(1, slows):
            fold_got(d).wait_recv()
            for e in range(1, fast):
                fold_cross(d, e).start()
        lax.fori_loop(3, reduced, slot, 0)
        for d in range(slows):
            for e in range(1, fast):
                fold_crossed(d, e).wait_recv()
        lax.fori_loop(reduced, summed, slot, 0)

        @pl.when(me == home)
        def _():
            for d in range(1, rows):
                token_copy(d - 1).wait_recv()
            total = t_ref[...]
            for d in range(1, rows):
                total += tbuf[d - 1]
            logit_ref[...] += total

        @pl.when(me != home)
        def _():
            token_copy(away - 1).wait_send()

        @pl.when(owning)
        def _():
            for d in range(1, cols):
                logit_copy(d).start()
            lbuf[col] = logit_ref[...]

        turned[...] = jnp.transpose(x_ref[...])
        lax.fori_loop(summed, summed + 1, slot, 0)

        @pl.when(owning)
        def _():
            for d in range(1, cols):
                logit_got(d).wait_recv()
            logits = lbuf[0]
            for c in range(1, cols):
                logits += lbuf[c]
            onehot_here = h_ref[mine].astype(F32)
            exponent = jnp.exp(logits)
            partition = jnp.sum(exponent, axis=1, keepdims=True)
            grads[mine] = (loss_scale * (exponent / partition - onehot_here)).astype(BF16)
            for d in range(1, rows):
                grad_copy(d).start()

            @pl.when(mine == col)
            def _():
                cost = jnp.log(partition) - jnp.sum(logits * onehot_here, axis=1, keepdims=True)
                loss_ref[...] = jnp.transpose(jnp.broadcast_to(cost, (share, 128)))[:8]
                for d in range(1, rows):
                    loss_copy(d).start()

        lax.fori_loop(summed + 1, ready, slot, 0)
        for q in range(owners):
            level = q if q < fast else q + (slows - 2) * fast

            @pl.when(me != level)
            def _(q=q):
                grad_got(q).wait_recv()

        dmixed[...] = dot(grads[...].reshape(tokens, classes), c_ref[...], 1, 1).astype(BF16)

        def catch_up(i, carry):
            slot(ready + i, 0)
            consume(2 * i)
            consume(2 * i + 1)
            return carry

        def keep_up(s, carry):
            slot(s, 0)
            consume(s - arrived)
            return carry

        lax.fori_loop(0, backlog, catch_up, 0)
        lax.fori_loop(ready + backlog, arrived + tiles, keep_up, 0)

        cparts[...] = acc[...].astype(BF16).reshape(cols, mine_rows, depth)
        _, slow, quick, _ = grid_of("col", pairs, cols)
        order = [(d, s) for s in range(slices) for d in [*range(1, far_cols), 0]]
        other = lax.rem(quick + 1, pairs)
        ccopies, dcopies = {}, {}
        for d, s in order:
            a = lax.rem(slow + d, far_cols)
            at = pl.ds(s * span, span)
            ccopies[d, s] = to(
                cparts.at[a * pairs + other, at], cx.at[d, at], cx_sems, d * slices + s, col=slow * pairs + other
            )
            ccopies[d, s].start()
        for d, s in order:
            a = lax.rem(slow + d, far_cols)
            at = pl.ds(s * span, span)
            ccopies[d, s].wait_recv()
            if d:
                total = cparts[a * pairs + quick, at].astype(F32) + cx[d, at].astype(F32)
                cy[d - 1, at] = total.astype(BF16)
                dcopies[d, s] = to(
                    cy.at[d - 1, at], cz.at[d - 1, at], cz_sems, (d - 1) * slices + s, col=a * pairs + quick
                )
                dcopies[d, s].start()
        for s in range(slices):
            at = pl.ds(s * span, span)
            own_rows = pl.ds(pl.multiple_of(col * mine_rows + s * span, 16), span)
            total = cparts[col, at].astype(F32) + cx[0, at].astype(F32) + dmixed[own_rows].astype(F32)
            for d in range(1, far_cols):
                dcopies[d, s].wait_recv()
                total += cz[d - 1, at].astype(F32)
            tg_ref[at] = total.astype(BF16)
        for copy in [*ccopies.values(), *dcopies.values()]:
            copy.wait_send()

        @pl.when(me != home)
        def _():
            loss_copy(1).wait_recv()

        @pl.when(me == home)
        def _():
            for d in range(1, rows):
                loss_copy(d).wait_send()

        @pl.when(owning)
        def _():
            for d in range(1, cols):
                logit_copy(d).wait_send()
            for d in range(1, rows):
                grad_copy(d).wait_send()

        for d in range(1, slows):
            fold_hop(d).wait_send()
        for d in range(slows):
            for e in range(1, fast):
                fold_cross(d, e).wait_send()
        for t in range(max(tiles - 2, 0), tiles):
            for copy in results(t):
                copy.wait()

        def drain(t, carry):
            for end in range(ENDS):
                _, towards, own, far = chain(end, z, slows)
                for e in range(1, fast):
                    gate_sum_cross(t, end, e).wait_send()

                @pl.when(jnp.logical_not(own))
                def _(end=end, towards=towards):
                    gate_sum_hop(t, end, towards).wait_send()
                    up_sum_hop(t, end, towards).wait_send()

                @pl.when(own)
                def _(end=end):
                    for e in range(1, fast):
                        up_sum_cross(t, end, e).wait_send()

            for end in range(ENDS):
                _, towards, own, far = chain(end, z, slows)
                for e in range(1, fast):
                    gate_cross(t, end, e).wait_send()

                @pl.when(jnp.logical_not(far))
                def _(end=end, towards=towards):
                    gate_hop(t, end, towards).wait_send()
                    up_hop(t, end, towards).wait_send()

                @pl.when(own)
                def _(end=end):
                    for e in range(1, fast):
                        up_cross(t, end, e).wait_send()

            return carry

        lax.fori_loop(0, tiles, drain, 0)

    vmem = pl.BlockSpec(memory_space=pltpu.VMEM)
    hbm = pl.BlockSpec(memory_space=pl.ANY)
    return pl.pallas_call(
        body,
        in_specs=[vmem, vmem, hbm, hbm, vmem, vmem, vmem, vmem, vmem],
        out_specs=[hbm, hbm, vmem, vmem, vmem, vmem],
        out_shape=[
            jax.ShapeDtypeStruct((2, tiles, tokens, step), BF16),
            jax.ShapeDtypeStruct((tiles, step, tokens), BF16),
            jax.ShapeDtypeStruct((depth, tokens), BF16),
            jax.ShapeDtypeStruct((tokens, depth), BF16),
            jax.ShapeDtypeStruct((mine_rows, depth), BF16),
            jax.ShapeDtypeStruct((8, share), F32),
        ],
        scratch_shapes=[
            pltpu.VMEM((2, tiles, depth, step), BF16),
            pltpu.VMEM((2, tiles, owners, share, step), BF16),
            pltpu.VMEM((tiles, ENDS, fast - 1, share, step), BF16),
            pltpu.VMEM((tiles, ENDS, share, step), BF16),
            pltpu.VMEM((tiles, ENDS, fast, share, step), BF16),
            pltpu.VMEM((tiles, fast - 1, share, step), BF16),
            pltpu.VMEM((tiles, share, step), F32),
            pltpu.VMEM((rows - 1, share, classes), F32),
            pltpu.VMEM((share, classes), F32),
            pltpu.VMEM((width, classes), BF16),
            pltpu.VMEM((2, 2, tokens, step), BF16),
            pltpu.VMEM((2, step, tokens), BF16),
            pltpu.VMEM((2, tiles, owners, share, step), BF16),
            pltpu.VMEM((owners, share, classes), BF16),
            pltpu.VMEM((cols, share, classes), F32),
            pltpu.VMEM((tokens, step), BF16),
            pltpu.VMEM((tokens, depth), F32),
            pltpu.VMEM((cols, mine_rows, depth), BF16),
            pltpu.VMEM((far_cols, mine_rows, depth), BF16),
            pltpu.VMEM((far_cols - 1, mine_rows, depth), BF16),
            pltpu.VMEM((far_cols - 1, mine_rows, depth), BF16),
            *both(tiles, ENDS, fast - 1),
            *both(tiles, ENDS),
            *both(tiles, ENDS),
            *both(tiles, fast - 1),
            *both(rows - 1),
            *both(slows - 1),
            *both(slows, fast - 1),
            *both(tiles, ENDS),
            *both(tiles, ENDS, fast - 1),
            *both(tiles, ENDS),
            *both(tiles, fast - 1),
            *both(cols - 1),
            pltpu.SemaphoreType.DMA((rows - 1,)),
            pltpu.SemaphoreType.DMA((owners,)),
            pltpu.SemaphoreType.DMA((rows - 1,)),
            pltpu.SemaphoreType.DMA((1,)),
            *both(far_cols * slices),
            *both((far_cols - 1) * slices),
            pltpu.SemaphoreType.DMA((2, tiles)),
            pltpu.SemaphoreType.DMA((3, tiles)),
        ],
        compiler_params=talking(call_id),
    )(x_all, onehot, gate, up, gate_mask, up_mask, fold_part, token_logits, head)


def shards(
    rows, cols, tokens, gate_weight, up_weight, down_weight, gate_mask, up_mask, down_mask, head_weight, labels
):
    classes = head_weight.shape[1]
    every_token, every_onehot, fold, gate_tiles, up_tiles, down_tiles, token_part = prepare(
        tokens,
        labels,
        down_weight,
        (gate_mask, up_mask, down_mask),
        head_weight,
        width_of_step(gate_weight.shape[1]),
        rows,
        cols,
        1,
    )
    deltas, hidden, turned, dmixed, tokens_grad, losses = layer(
        every_token,
        every_onehot.reshape(cols, -1, classes),
        gate_weight,
        up_weight,
        gate_tiles,
        up_tiles,
        fold,
        token_part,
        head_weight,
        rows,
        cols,
        2,
    )
    gate_grad, up_grad, down_grad = weight_grads(turned, deltas, hidden, dmixed, gate_tiles, up_tiles, down_tiles)
    return (losses[0], tokens_grad, gate_grad, up_grad, down_grad)


def solution(mesh):
    placed = (
        P("col", "row"),
        P("row", "col"),
        P("row", "col"),
        P("col", "row"),
        P("row", "col"),
        P("row", "col"),
        P("col", "row"),
        P("row", None),
        P("col"),
    )
    return jax.shard_map(
        functools.partial(shards, mesh.shape["row"], mesh.shape["col"]),
        mesh=mesh,
        in_specs=placed,
        out_specs=(P("col"), P("col", "row"), P("row", "col"), P("row", "col"), P("col", "row")),
        check_vma=False,
    )
```

```python
import functools

import jax
import jax.numpy as jnp
from jax import lax
from jax.experimental import pallas as pl
from jax.experimental.pallas import tpu as pltpu
from jax.sharding import PartitionSpec as P

loss_scale = 8.0
F32 = jnp.float32
BF16 = jnp.bfloat16
MESH = pl.DeviceIdType.MESH


def tile_of(width):
    for tile in (512, 256, 128):
        if width % tile == 0:
            return tile
    return width


def pruned(values, mask):
    height, breadth = values.shape
    blocks = mask.shape[0]
    split = values.reshape(blocks, height // blocks, breadth)
    kept = split * mask[:, None, :].astype(values.dtype)
    return kept.reshape(height, breadth)


def dot(a, b, a_axis, b_axis):
    return lax.dot_general(a, b, (((a_axis,), (b_axis,)), ((), ())), preferred_element_type=F32)


def run(body, grid, in_specs, out_specs, out_shape, flops, touched, scratch=()):
    return pl.pallas_call(
        body,
        grid=grid,
        in_specs=in_specs,
        out_specs=out_specs,
        out_shape=out_shape,
        scratch_shapes=list(scratch),
        compiler_params=pltpu.CompilerParams(vmem_limit_bytes=60 << 20),
        cost_estimate=pl.CostEstimate(flops=flops, bytes_accessed=touched, transcendentals=0),
    )


def weight_grads(turned, deltas, hidden, dmixed, gate_mask, up_mask, down_mask):
    _, tiles, tokens, step = deltas.shape
    depth = turned.shape[0]
    width = tiles * step
    steps = down_mask.shape[0]
    pair = tiles // steps
    span = pair * step
    blocks = gate_mask.shape[1]

    def body(x_ref, d_ref, h_ref, m_ref, gm_ref, um_ref, dm_ref, gg_ref, ug_ref, dg_ref):
        for i in range(pair):
            at = slice(i * step, (i + 1) * step)
            for k, (mask, out) in enumerate(((gm_ref, gg_ref), (um_ref, ug_ref))):
                out[:, at] = pruned(dot(x_ref[...], d_ref[k, i], 1, 0).astype(BF16), mask[i])
        dg_ref[...] = pruned(dot(h_ref[...].reshape(span, tokens), m_ref[...], 1, 0).astype(BF16), dm_ref[0])

    weight = pl.BlockSpec((depth, span), lambda j: (0, j))
    mask = pl.BlockSpec((pair, blocks, step), lambda j: (j, 0, 0))
    return run(
        body,
        (steps,),
        [
            pl.BlockSpec((depth, tokens), lambda j: (0, 0)),
            pl.BlockSpec((2, pair, tokens, step), lambda j: (0, j, 0, 0)),
            pl.BlockSpec((pair, step, tokens), lambda j: (j, 0, 0)),
            pl.BlockSpec((tokens, depth), lambda j: (0, 0)),
            mask,
            mask,
            pl.BlockSpec((1, down_mask.shape[1], depth), lambda j: (j, 0, 0)),
        ],
        [weight, weight, pl.BlockSpec((span, depth), lambda j: (j, 0))],
        [
            jax.ShapeDtypeStruct((depth, width), BF16),
            jax.ShapeDtypeStruct((depth, width), BF16),
            jax.ShapeDtypeStruct((width, depth), BF16),
        ],
        6 * tokens * depth * width,
        10 * depth * width,
    )(turned, deltas, hidden, dmixed, gate_mask, up_mask, down_mask)


def grid_of(axis, fast, size):
    me = lax.axis_index(axis)
    return me, lax.div(me, fast), lax.rem(me, fast), size // fast


def talking(call_id):
    return pltpu.CompilerParams(
        collective_id=call_id, has_side_effects=True, vmem_limit_bytes=60 << 20
    )


def both(*dims):
    return [pltpu.SemaphoreType.DMA(dims), pltpu.SemaphoreType.DMA(dims)]


ENDS = 2
LAG = 2
LAG_CROSS = 1


def place(rows):
    fast = rows // 4
    me, z, x, slows = grid_of("row", fast, rows)
    return me, z, x, fast, slows


def chain(end, z, slows):
    if end:
        return slows - 1 - z, 1, z == slows - 1, z == 0
    return z, -1, z == 0, z == slows - 1


def owner_row(block, fast, slows):
    return jnp.where(block < fast, block, block + (slows - 2) * fast)


def greet_rows(rows, cols=None):
    barrier = pltpu.get_barrier_semaphore()
    me = lax.axis_index("row")
    for d in range(1, rows):
        pl.semaphore_signal(barrier, inc=1, device_id={"row": lax.rem(me + d, rows)}, device_id_type=MESH)
    total = rows - 1
    if cols is not None:
        mine = lax.axis_index("col")
        for d in range(1, cols):
            pl.semaphore_signal(barrier, inc=1, device_id={"col": lax.rem(mine + d, cols)}, device_id_type=MESH)
        total += cols - 1
    pl.semaphore_wait(barrier, total)


def to(src, dst, sems, at, **there):
    return pltpu.make_async_remote_copy(
        src_ref=src,
        dst_ref=dst,
        send_sem=sems[0].at[at],
        recv_sem=sems[1].at[at],
        device_id=there,
        device_id_type=MESH,
    )


def by_rows(count, step, work):
    def go(i, carry):
        work(pl.ds(pl.multiple_of(i * step, step), step))
        return carry

    lax.fori_loop(0, count // step, go, 0)


def width_of_step(width):
    return 256 if width % 256 == 0 else 128


def prepare(tokens, labels, down, masks, head, step, rows, cols, call_id):
    mine, depth = tokens.shape
    width, classes = down.shape[0], head.shape[1]
    tile = tile_of(width)
    steps = width // tile
    tiles = width // step
    gate_mask, up_mask, down_mask = masks
    blocks = gate_mask.shape[0]
    down_mask = down_mask.reshape(steps, -1, down_mask.shape[1])
    fast, slows = rows // 4, 4
    pairs, far = 2, cols // 2
    piece = width // rows
    slices = next(n for n in (4, 7, 2, 1) if piece % (16 * n) == 0)
    span = piece // slices
    halves = 2
    half = mine // halves

    def stretch(mask, first, span, out):
        lanes = out // mask.shape[1]
        kind = (mask.shape[1], span)
        source = lax.broadcasted_iota(jnp.int32, kind, 0)
        target = lax.div(first + lax.broadcasted_iota(jnp.int32, kind, 1), lanes)
        pick = (source == target).astype(F32).astype(BF16)
        return dot(mask.astype(F32).astype(BF16), pick, 1, 0)

    def body(
        x_ref, l_ref, w_hbm, gm_ref, um_ref, m_ref, c_ref,
        x_all, h_all, fold, gate_out, up_out, down_out, token_out,
        h_ref, weights, parts, xbuf, ybuf, zbuf, *sems,
    ):
        xs, zs, cx, cz = (sems[2 * i : 2 * i + 2] for i in range(4))
        w_sems, local = sems[8], sems[9]
        me, z, x, _, _ = place(rows)
        col, slow, quick, _ = grid_of("col", pairs, cols)

        def fetch(t):
            cut = pl.ds(pl.multiple_of(t * tile, tile), tile)
            return pltpu.make_async_copy(w_hbm.at[cut], weights.at[t], w_sems.at[t])

        def start_fetch(t, carry):
            fetch(t).start()
            return carry

        lax.fori_loop(0, steps, start_fetch, 0)
        greet_rows(rows, cols)
        started = []

        def go(copy):
            copy.start()
            started.append(copy)
            return copy

        number = jnp.broadcast_to(l_ref[...], (classes, mine))
        turned = (number == lax.broadcasted_iota(jnp.int32, (classes, mine), 0)).astype(F32)
        h_ref[...] = jnp.transpose(turned).astype(BF16)
        ins, outs = (x_ref, h_ref), (x_all, h_all)
        arrivals = {}

        def across(k, s, d, src, block):
            cut = pl.ds(s * half, half)
            return go(
                to(src, outs[k].at[block, cut], cx, ((k * halves + s) * far + d), col=slow * pairs + lax.rem(quick + 1, pairs))
            )

        for s in range(halves):
            for k in range(2):
                cut = pl.ds(s * half, half)
                for d in range(1, far):
                    there = lax.rem(slow + d, far) * pairs + quick
                    arrivals[k, s, d] = go(
                        to(ins[k].at[cut], outs[k].at[col, cut], cz, ((k * halves + s) * (far - 1) + d - 1), col=there)
                    )
                across(k, s, 0, ins[k].at[cut], col)
        keep = [pltpu.make_async_copy(ins[k], outs[k].at[col], local.at[k]) for k in range(2)]
        for copy in keep:
            copy.start()

        def fold_tile(t, carry):
            fetch(t).wait()
            cut = pl.ds(pl.multiple_of(t * tile, tile), tile)
            down_out[t] = stretch(m_ref[t], 0, depth, depth)
            parts[cut] = dot(pruned(weights[t], down_out[t]), c_ref[...], 1, 0).astype(BF16)
            return carry

        lax.fori_loop(0, steps, fold_tile, 0)

        def rows_of(block, s):
            return pl.ds(pl.multiple_of(block * piece + s * span, 16), span)

        order = [(d, s) for s in range(slices) for d in [*range(1, slows), 0]]
        xcopies, zcopies = {}, {}
        for d, s in order:
            a = lax.rem(z + d, slows)
            for e in range(1, fast):
                b = lax.rem(x + e, fast)
                xcopies[d, s, e] = go(
                    to(
                        parts.at[rows_of(a * fast + b, s)],
                        xbuf.at[e - 1, d, pl.ds(s * span, span)],
                        xs,
                        (d * slices + s) * (fast - 1) + e - 1,
                        row=z * fast + b,
                    )
                )

        def widen(t, carry):
            for mask, out in ((gm_ref, gate_out), (um_ref, up_out)):
                out[t] = stretch(mask[...], t * step, step, width)
            return carry

        lax.fori_loop(0, tiles, widen, 0)
        token_out[...] = dot(x_ref[...], c_ref[...], 1, 0)

        for s in range(halves):
            for k in range(2):
                for d in range(1, far):
                    there = lax.rem(slow + far - d, far) * pairs + quick
                    arrivals[k, s, d].wait_recv()
                    across(k, s, d, outs[k].at[there, pl.ds(s * half, half)], there)

        for d, s in order:
            a = lax.rem(z + d, slows)
            for e in range(1, fast):
                xcopies[d, s, e].wait_recv()
            at = pl.ds(s * span, span)
            total = parts[rows_of(a * fast + x, s)].astype(F32)
            for e in range(1, fast):
                total += xbuf[e - 1, d, at].astype(F32)
            if d:
                ybuf[d - 1, at] = total.astype(BF16)
                zcopies[d, s] = go(
                    to(ybuf.at[d - 1, at], zbuf.at[d - 1, at], zs, (d - 1) * slices + s, row=a * fast + x)
                )
            else:
                parts[rows_of(a * fast + x, s)] = total.astype(BF16)

        for s in range(slices):
            at = pl.ds(s * span, span)
            for d in range(1, slows):
                zcopies[d, s].wait_recv()
            total = parts[rows_of(me, s)].astype(F32)
            for d in range(1, slows):
                total += zbuf[d - 1, at].astype(F32)
            fold[at] = total.astype(BF16)
        received = {id(c) for c in [*xcopies.values(), *zcopies.values(), *arrivals.values()]}
        for copy in started:
            copy.wait_send()
            if id(copy) not in received:
                copy.wait_recv()
        for copy in keep:
            copy.wait()

    vmem = pl.BlockSpec(memory_space=pltpu.VMEM)
    got = pl.pallas_call(
        body,
        in_specs=[vmem, vmem, pl.BlockSpec(memory_space=pl.ANY), vmem, vmem, vmem, vmem],
        out_specs=[vmem] * 7,
        out_shape=[
            jax.ShapeDtypeStruct((cols, mine, depth), BF16),
            jax.ShapeDtypeStruct((cols, mine, classes), BF16),
            jax.ShapeDtypeStruct((piece, classes), BF16),
            jax.ShapeDtypeStruct((tiles, blocks, step), F32),
            jax.ShapeDtypeStruct((tiles, blocks, step), F32),
            jax.ShapeDtypeStruct((steps, down_mask.shape[1], depth), F32),
            jax.ShapeDtypeStruct((mine, classes), F32),
        ],
        scratch_shapes=[
            pltpu.VMEM((mine, classes), BF16),
            pltpu.VMEM((steps, tile, depth), BF16),
            pltpu.VMEM((width, classes), BF16),
            pltpu.VMEM((fast - 1, slows, piece, classes), BF16),
            pltpu.VMEM((slows - 1, piece, classes), BF16),
            pltpu.VMEM((slows - 1, piece, classes), BF16),
            *both(slows * slices * (fast - 1)),
            *both((slows - 1) * slices),
            *both(2 * halves * far),
            *both(2 * halves * (far - 1)),
            pltpu.SemaphoreType.DMA((steps,)),
            pltpu.SemaphoreType.DMA((2,)),
        ],
        compiler_params=talking(call_id),
    )(tokens, labels.reshape(1, mine), down, gate_mask, up_mask, down_mask, head)
    return got[0].reshape(-1, depth), got[1].reshape(-1, classes), *got[2:]


def layer(x_all, onehot, gate, up, gate_mask, up_mask, fold_part, token_logits, head, rows, cols, call_id):
    tokens, depth = x_all.shape
    width = gate.shape[1]
    tiles, blocks, step = gate_mask.shape
    piece, classes = fold_part.shape
    fast, slows = rows // 4, 4
    owners = ENDS * fast
    share = tokens // owners
    group = 32
    mine_rows = tokens // cols
    hops_all = LAG * (slows - 1)
    reduced = 2 * LAG_CROSS + hops_all
    begin = max(tiles, reduced)
    arrived = begin + hops_all + LAG_CROSS
    summed = tiles + reduced
    ready = summed + 3
    backlog = max(ready - arrived, 0)

    def body(
        x_ref, h_ref, g_hbm, u_hbm, gm_ref, um_ref, p_ref, t_ref, c_ref,
        deltas_hbm, hidden_hbm, turned, dmixed, loss_ref, kept_ref, *rest,
    ):
        sent, rest = rest[: cols - 1], rest[cols - 1 :]
        (
            weights, parts, xa, za, zb, xb, gates, tbuf, logit_ref, fold,
            deltas, hidden_ref, all_ref, grads, lbuf, hbuf, acc,
        ) = rest[:17]
        sems = rest[17:]
        (
            xa_sems, za_sems, zb_sems, xb_sems, t_sems, fz_sems, fx_sems,
            gza_sems, gxa_sems, gzb_sems, gxb_sems, l_sems, d_sems, loss_sems,
        ) = (sems[2 * i : 2 * i + 2] for i in range(14))
        w_sems, out_sems = sems[28:]
        me, z, x, _, _ = place(rows)
        col = lax.axis_index("col")
        mine = jnp.where(z == 0, x, fast + x)
        owning = jnp.logical_or(z == 0, z == slows - 1)

        def fetch(t, k):
            cut = pl.ds(pl.multiple_of(t * step, step), step)
            return pltpu.make_async_copy((g_hbm, u_hbm)[k].at[:, cut], weights.at[k, t], w_sems.at[k, t])

        def start_fetch(t, carry):
            for k in range(2):
                fetch(t, k).start()
            return carry

        lax.fori_loop(0, tiles, start_fetch, 0)
        greet_rows(rows, cols)

        def fold_rows(t):
            return pl.ds(pl.multiple_of(t * step, step), step)

        def fold_block(row):
            return fold.at[pl.ds(pl.multiple_of(row * piece, 16), piece)]

        def ring(t):
            return lax.rem(t, 2)

        def fold_hop(d):
            return to(p_ref, fold_block(me), fz_sems, d - 1, row=lax.rem(z + d, slows) * fast + x)

        def fold_got(d):
            block = fold_block(lax.rem(z + slows - d, slows) * fast + x)
            return to(block, block, fz_sems, d - 1, row=lax.rem(z + d, slows) * fast + x)

        def fold_cross(d, e):
            block = fold_block(lax.rem(z + slows - d, slows) * fast + x)
            return to(block, block, fx_sems, (d, e - 1), row=z * fast + lax.rem(x + e, fast))

        def fold_crossed(d, e):
            block = fold_block(lax.rem(z + slows - d, slows) * fast + lax.rem(x + fast - e, fast))
            return to(block, block, fx_sems, (d, e - 1), row=z * fast + lax.rem(x + e, fast))

        def gate_sum_cross(t, end, e):
            there = lax.rem(x + e, fast)
            return to(parts.at[0, t, end * fast + there], xa.at[t, end, e - 1], xa_sems, (t, end, e - 1), row=z * fast + there)

        def gate_sum_hop(t, end, towards):
            return to(parts.at[0, t, end * fast + x], za.at[t, end], za_sems, (t, end), row=(z + towards) * fast + x)

        def up_sum_hop(t, end, towards):
            return to(parts.at[1, t, pl.ds(end * fast, fast)], zb.at[t, end], zb_sems, (t, end), row=(z + towards) * fast + x)

        def up_sum_cross(t, end, e):
            there = lax.rem(x + e, fast)
            return to(parts.at[1, t, end * fast + there], xb.at[t, e - 1], xb_sems, (t, e - 1), row=z * fast + there)

        home = owner_row(col, fast, slows)
        away = lax.rem(me - home + rows, rows)

        def token_copy(slot):
            return to(t_ref, tbuf.at[slot], t_sems, slot, row=home)

        @pl.when(me != home)
        def _():
            token_copy(away - 1).start()

        for d in range(1, slows):
            fold_hop(d).start()
        fold[pl.ds(pl.multiple_of(me * piece, 16), piece)] = p_ref[...]
        for e in range(1, fast):
            fold_cross(0, e).start()
        logit_ref[...] = jnp.zeros_like(logit_ref)
        acc[...] = jnp.zeros_like(acc)

        def reduce_slot(s):
            @pl.when(s < tiles)
            def _():
                t = s
                for k, m in enumerate((gm_ref, um_ref)):
                    fetch(t, k).wait()
                    part = dot(x_ref[...], pruned(weights[k, t], m[t]), 1, 0).astype(BF16)
                    parts[k, t] = part.reshape(owners, share, step)
                    for end in range(ENDS):
                        if k == 0:
                            for e in range(1, fast):
                                gate_sum_cross(t, end, e).start()
                        else:
                            _, towards, _, far = chain(end, z, slows)

                            @pl.when(far)
                            def _(end=end, towards=towards):
                                up_sum_hop(t, end, towards).start()

            for end in range(ENDS):
                hops, towards, own, far = chain(end, z, slows)
                t = s - LAG_CROSS - LAG * (slows - 1 - hops)
                inside = jnp.logical_and(t >= 0, t < tiles)

                @pl.when(inside)
                def _(end=end, t=t, towards=towards, own=own, far=far):
                    at = end * fast + x
                    for e in range(1, fast):
                        gate_sum_cross(t, end, e).wait_recv()

                    @pl.when(far)
                    def _():
                        def add(cut):
                            total = parts[0, t, at, cut].astype(F32)
                            for e in range(1, fast):
                                total += xa[t, end, e - 1, cut].astype(F32)
                            parts[0, t, at, cut] = total.astype(BF16)

                        by_rows(share, group, add)

                    @pl.when(jnp.logical_not(far))
                    def _():
                        gate_sum_hop(t, end, towards).wait_recv()

                        def add(cut):
                            total = parts[0, t, at, cut].astype(F32) + za[t, end, cut].astype(F32)
                            for e in range(1, fast):
                                total += xa[t, end, e - 1, cut].astype(F32)
                            parts[0, t, at, cut] = total.astype(BF16)

                            @pl.when(own)
                            def _():
                                gates[t, cut] = total

                        by_rows(share, group, add)

                    @pl.when(jnp.logical_not(own))
                    def _():
                        gate_sum_hop(t, end, towards).start()

                    @pl.when(jnp.logical_not(far))
                    def _():
                        up_sum_hop(t, end, towards).wait_recv()

                        def add_block(b):
                            def add(cut):
                                total = parts[1, t, end * fast + b, cut].astype(F32) + zb[t, end, b, cut].astype(F32)
                                parts[1, t, end * fast + b, cut] = total.astype(BF16)

                            by_rows(share, group, add)

                        @pl.when(jnp.logical_not(own))
                        def _():
                            for b in range(fast):
                                add_block(b)
                            up_sum_hop(t, end, towards).start()

                        @pl.when(own)
                        def _():
                            for e in range(1, fast):
                                add_block(lax.rem(x + e, fast))
                                up_sum_cross(t, end, e).start()

            for end in range(ENDS):
                _, _, own, _ = chain(end, z, slows)
                t = s - 2 * LAG_CROSS - LAG * (slows - 1)
                done = jnp.logical_and(own, jnp.logical_and(t >= 0, t < tiles))

                @pl.when(done)
                def _(end=end, t=t):
                    for e in range(1, fast):
                        up_sum_cross(t, end, e).wait_recv()

                    def close(cut):
                        up_sum = parts[1, t, end * fast + x, cut].astype(F32) + zb[t, end, x, cut].astype(F32)
                        for e in range(1, fast):
                            up_sum += xb[t, e - 1, cut].astype(F32)
                        gate_sum = gates[t, cut]
                        all_ref[0, t, mine, cut] = gate_sum.astype(BF16)
                        all_ref[1, t, mine, cut] = up_sum.astype(BF16)
                        hidden = (gate_sum * jax.nn.sigmoid(gate_sum) * up_sum).astype(BF16)
                        logit_ref[cut] += dot(hidden, fold[fold_rows(t)], 1, 0)

                    by_rows(share, share, close)


        def gate_hop(t, end, towards):
            q = end * fast + x
            return to(all_ref.at[0, t, q], all_ref.at[0, t, q], gza_sems, (t, end), row=(z - towards) * fast + x)

        def gate_cross(t, end, e):
            q = end * fast + x
            return to(all_ref.at[0, t, q], all_ref.at[0, t, q], gxa_sems, (t, end, e - 1), row=z * fast + lax.rem(x + e, fast))

        def gate_got(t, end, e):
            q = end * fast + lax.rem(x + fast - e, fast)
            return to(all_ref.at[0, t, q], all_ref.at[0, t, q], gxa_sems, (t, end, e - 1), row=z * fast + lax.rem(x + e, fast))

        def up_hop(t, end, towards):
            cut = pl.ds(end * fast, fast)
            return to(all_ref.at[1, t, cut], all_ref.at[1, t, cut], gzb_sems, (t, end), row=(z - towards) * fast + x)

        def up_cross(t, end, e):
            q = end * fast + x
            return to(all_ref.at[1, t, q], all_ref.at[1, t, q], gxb_sems, (t, e - 1), row=z * fast + lax.rem(x + e, fast))

        def up_got(t, end, e):
            q = end * fast + lax.rem(x + fast - e, fast)
            return to(all_ref.at[1, t, q], all_ref.at[1, t, q], gxb_sems, (t, e - 1), row=z * fast + lax.rem(x + e, fast))

        def logit_copy(d):
            return to(logit_ref, lbuf.at[col], l_sems, d - 1, col=lax.rem(col + d, cols))

        def logit_got(d):
            return to(logit_ref, lbuf.at[lax.rem(col + cols - d, cols)], l_sems, d - 1, col=lax.rem(col + d, cols))

        def grad_copy(d):
            there = lax.rem(me + d, rows)
            return pltpu.make_async_remote_copy(
                src_ref=grads.at[mine],
                dst_ref=grads.at[mine],
                send_sem=d_sems[0].at[d - 1],
                recv_sem=d_sems[1].at[mine],
                device_id={"row": there},
                device_id_type=MESH,
            )

        def grad_got(q):
            return pltpu.make_async_remote_copy(
                src_ref=grads.at[q],
                dst_ref=grads.at[q],
                send_sem=d_sems[0].at[0],
                recv_sem=d_sems[1].at[q],
                device_id={"row": lax.rem(me + 1, rows)},
                device_id_type=MESH,
            )

        def loss_copy(d):
            return pltpu.make_async_remote_copy(
                src_ref=loss_ref,
                dst_ref=loss_ref,
                send_sem=loss_sems[0].at[d - 1],
                recv_sem=loss_sems[1].at[0],
                device_id={"row": lax.rem(me + d, rows)},
                device_id_type=MESH,
            )

        def gather_slot(s):
            for end in range(ENDS):
                hops, towards, own, far = chain(end, z, slows)
                t = s - LAG * hops

                @pl.when(jnp.logical_and(t >= 0, t < tiles))
                def _(end=end, t=t, towards=towards, own=own, far=far):
                    @pl.when(jnp.logical_not(own))
                    def _():
                        gate_hop(t, end, towards).wait_recv()

                    @pl.when(jnp.logical_not(far))
                    def _():
                        gate_hop(t, end, towards).start()

                    for e in range(1, fast):
                        gate_cross(t, end, e).start()

                    @pl.when(own)
                    def _():
                        for e in range(1, fast):
                            up_cross(t, end, e).start()

                t = s - LAG * hops - LAG_CROSS

                @pl.when(jnp.logical_and(t >= 0, t < tiles))
                def _(end=end, t=t, towards=towards, own=own, far=far):
                    @pl.when(own)
                    def _():
                        for e in range(1, fast):
                            up_got(t, end, e).wait_recv()

                    @pl.when(jnp.logical_not(own))
                    def _():
                        up_hop(t, end, towards).wait_recv()

                    @pl.when(jnp.logical_not(far))
                    def _():
                        up_hop(t, end, towards).start()

        def results(t):
            return (
                pltpu.make_async_copy(deltas.at[ring(t), 0], deltas_hbm.at[0, t], out_sems.at[0, t]),
                pltpu.make_async_copy(deltas.at[ring(t), 1], deltas_hbm.at[1, t], out_sems.at[1, t]),
                pltpu.make_async_copy(hidden_ref.at[ring(t)], hidden_hbm.at[t], out_sems.at[2, t]),
            )

        def consume(t):
            for end in range(ENDS):
                for e in range(1, fast):
                    gate_got(t, end, e).wait_recv()

            @pl.when(t >= 2)
            def _():
                for copy in results(t - 2):
                    copy.wait()

            def delta(q, carry):
                at = pl.ds(pl.multiple_of(q * share, share), share)
                dhidden = dot(grads[q], fold[fold_rows(t)], 1, 1)
                gate_sum = all_ref[0, t, q].astype(F32)
                up_sum = all_ref[1, t, q].astype(F32)
                sigmoid_gate = jax.nn.sigmoid(gate_sum)
                activated = gate_sum * sigmoid_gate
                hbuf[at] = (activated * up_sum).astype(BF16)
                slope = sigmoid_gate * (1.0 + gate_sum * (1.0 - sigmoid_gate))
                deltas[ring(t), 0, at] = (dhidden * up_sum * slope).astype(BF16)
                deltas[ring(t), 1, at] = (dhidden * activated).astype(BF16)
                return carry

            lax.fori_loop(0, owners, delta, 0)
            hidden_ref[ring(t)] = jnp.transpose(hbuf[...])
            for copy in results(t):
                copy.start()
            part = None
            for k, m in enumerate((gm_ref, um_ref)):
                term = dot(deltas[ring(t), k], pruned(weights[k, t], m[t]), 1, 1)
                part = term if part is None else part + term
            acc[...] += part

        def slot(s, carry):
            reduce_slot(s)
            gather_slot(s - begin)
            return carry

        lax.fori_loop(0, 3, slot, 0)
        for d in range(1, slows):
            fold_got(d).wait_recv()
            for e in range(1, fast):
                fold_cross(d, e).start()
        lax.fori_loop(3, reduced, slot, 0)
        for d in range(slows):
            for e in range(1, fast):
                fold_crossed(d, e).wait_recv()
        lax.fori_loop(reduced, summed, slot, 0)

        @pl.when(me == home)
        def _():
            for d in range(1, rows):
                token_copy(d - 1).wait_recv()
            total = t_ref[...]
            for d in range(1, rows):
                total += tbuf[d - 1]
            logit_ref[...] += total

        @pl.when(me != home)
        def _():
            token_copy(away - 1).wait_send()

        @pl.when(owning)
        def _():
            for d in range(1, cols):
                logit_copy(d).start()
            lbuf[col] = logit_ref[...]

        turned[...] = jnp.transpose(x_ref[...])
        lax.fori_loop(summed, summed + 1, slot, 0)

        @pl.when(owning)
        def _():
            for d in range(1, cols):
                logit_got(d).wait_recv()
            logits = lbuf[0]
            for c in range(1, cols):
                logits += lbuf[c]
            onehot_here = h_ref[mine].astype(F32)
            exponent = jnp.exp(logits)
            partition = jnp.sum(exponent, axis=1, keepdims=True)
            grads[mine] = (loss_scale * (exponent / partition - onehot_here)).astype(BF16)
            for d in range(1, rows):
                grad_copy(d).start()

            @pl.when(mine == col)
            def _():
                cost = jnp.log(partition) - jnp.sum(logits * onehot_here, axis=1, keepdims=True)
                loss_ref[...] = jnp.transpose(jnp.broadcast_to(cost, (share, 128)))[:8]
                for d in range(1, rows):
                    loss_copy(d).start()

        lax.fori_loop(summed + 1, ready, slot, 0)
        for q in range(owners):
            level = q if q < fast else q + (slows - 2) * fast

            @pl.when(me != level)
            def _(q=q):
                grad_got(q).wait_recv()

        dmixed[...] = dot(grads[...].reshape(tokens, classes), c_ref[...], 1, 1).astype(BF16)

        def catch_up(i, carry):
            slot(ready + i, 0)
            consume(2 * i)
            consume(2 * i + 1)
            return carry

        def keep_up(s, carry):
            slot(s, 0)
            consume(s - arrived)
            return carry

        lax.fori_loop(0, backlog, catch_up, 0)
        lax.fori_loop(ready + backlog, arrived + tiles, keep_up, 0)

        for d in range(cols):
            block = pl.ds(pl.multiple_of(lax.rem(col + d, cols) * mine_rows, mine_rows), mine_rows)
            if d:
                sent[d - 1][...] = acc[block].astype(BF16)
            else:
                kept_ref[...] = acc[block] + dmixed[block].astype(F32)

        @pl.when(me != home)
        def _():
            loss_copy(1).wait_recv()

        @pl.when(me == home)
        def _():
            for d in range(1, rows):
                loss_copy(d).wait_send()

        @pl.when(owning)
        def _():
            for d in range(1, cols):
                logit_copy(d).wait_send()
            for d in range(1, rows):
                grad_copy(d).wait_send()

        for d in range(1, slows):
            fold_hop(d).wait_send()
        for d in range(slows):
            for e in range(1, fast):
                fold_cross(d, e).wait_send()
        for t in range(max(tiles - 2, 0), tiles):
            for copy in results(t):
                copy.wait()

        def drain(t, carry):
            for end in range(ENDS):
                _, towards, own, far = chain(end, z, slows)
                for e in range(1, fast):
                    gate_sum_cross(t, end, e).wait_send()

                @pl.when(jnp.logical_not(own))
                def _(end=end, towards=towards):
                    gate_sum_hop(t, end, towards).wait_send()
                    up_sum_hop(t, end, towards).wait_send()

                @pl.when(own)
                def _(end=end):
                    for e in range(1, fast):
                        up_sum_cross(t, end, e).wait_send()

            for end in range(ENDS):
                _, towards, own, far = chain(end, z, slows)
                for e in range(1, fast):
                    gate_cross(t, end, e).wait_send()

                @pl.when(jnp.logical_not(far))
                def _(end=end, towards=towards):
                    gate_hop(t, end, towards).wait_send()
                    up_hop(t, end, towards).wait_send()

                @pl.when(own)
                def _(end=end):
                    for e in range(1, fast):
                        up_cross(t, end, e).wait_send()

            return carry

        lax.fori_loop(0, tiles, drain, 0)

    vmem = pl.BlockSpec(memory_space=pltpu.VMEM)
    hbm = pl.BlockSpec(memory_space=pl.ANY)
    return pl.pallas_call(
        body,
        in_specs=[vmem, vmem, hbm, hbm, vmem, vmem, vmem, vmem, vmem],
        out_specs=[hbm, hbm, *[vmem] * (3 + cols)],
        out_shape=[
            jax.ShapeDtypeStruct((2, tiles, tokens, step), BF16),
            jax.ShapeDtypeStruct((tiles, step, tokens), BF16),
            jax.ShapeDtypeStruct((depth, tokens), BF16),
            jax.ShapeDtypeStruct((tokens, depth), BF16),
            jax.ShapeDtypeStruct((8, share), F32),
            jax.ShapeDtypeStruct((mine_rows, depth), F32),
            *[jax.ShapeDtypeStruct((mine_rows, depth), BF16)] * (cols - 1),
        ],
        scratch_shapes=[
            pltpu.VMEM((2, tiles, depth, step), BF16),
            pltpu.VMEM((2, tiles, owners, share, step), BF16),
            pltpu.VMEM((tiles, ENDS, fast - 1, share, step), BF16),
            pltpu.VMEM((tiles, ENDS, share, step), BF16),
            pltpu.VMEM((tiles, ENDS, fast, share, step), BF16),
            pltpu.VMEM((tiles, fast - 1, share, step), BF16),
            pltpu.VMEM((tiles, share, step), F32),
            pltpu.VMEM((rows - 1, share, classes), F32),
            pltpu.VMEM((share, classes), F32),
            pltpu.VMEM((width, classes), BF16),
            pltpu.VMEM((2, 2, tokens, step), BF16),
            pltpu.VMEM((2, step, tokens), BF16),
            pltpu.VMEM((2, tiles, owners, share, step), BF16),
            pltpu.VMEM((owners, share, classes), BF16),
            pltpu.VMEM((cols, share, classes), F32),
            pltpu.VMEM((tokens, step), BF16),
            pltpu.VMEM((tokens, depth), F32),
            *both(tiles, ENDS, fast - 1),
            *both(tiles, ENDS),
            *both(tiles, ENDS),
            *both(tiles, fast - 1),
            *both(rows - 1),
            *both(slows - 1),
            *both(slows, fast - 1),
            *both(tiles, ENDS),
            *both(tiles, ENDS, fast - 1),
            *both(tiles, ENDS),
            *both(tiles, fast - 1),
            *both(cols - 1),
            pltpu.SemaphoreType.DMA((rows - 1,)),
            pltpu.SemaphoreType.DMA((owners,)),
            pltpu.SemaphoreType.DMA((rows - 1,)),
            pltpu.SemaphoreType.DMA((1,)),
            pltpu.SemaphoreType.DMA((2, tiles)),
            pltpu.SemaphoreType.DMA((3, tiles)),
        ],
        compiler_params=talking(call_id),
    )(x_all, onehot, gate, up, gate_mask, up_mask, fold_part, token_logits, head)


def shards(
    rows, cols, tokens, gate_weight, up_weight, down_weight, gate_mask, up_mask, down_mask, head_weight, labels
):
    classes = head_weight.shape[1]
    every_token, every_onehot, fold, gate_tiles, up_tiles, down_tiles, token_part = prepare(
        tokens,
        labels,
        down_weight,
        (gate_mask, up_mask, down_mask),
        head_weight,
        width_of_step(gate_weight.shape[1]),
        rows,
        cols,
        1,
    )
    deltas, hidden, turned, dmixed, losses, input_sum, *outgoing = layer(
        every_token,
        every_onehot.reshape(cols, -1, classes),
        gate_weight,
        up_weight,
        gate_tiles,
        up_tiles,
        fold,
        token_part,
        head_weight,
        rows,
        cols,
        2,
    )
    incoming = [
        lax.ppermute(block, "col", [(c, (c + d) % cols) for c in range(cols)])
        for d, block in enumerate(outgoing, 1)
    ]
    gate_grad, up_grad, down_grad = weight_grads(turned, deltas, hidden, dmixed, gate_tiles, up_tiles, down_tiles)
    for block in incoming:
        input_sum += block.astype(F32)
    tokens_grad = input_sum.astype(BF16)
    return (losses[0], tokens_grad, gate_grad, up_grad, down_grad)


def solution(mesh):
    placed = (
        P("col", "row"),
        P("row", "col"),
        P("row", "col"),
        P("col", "row"),
        P("row", "col"),
        P("row", "col"),
        P("col", "row"),
        P("row", None),
        P("col"),
    )
    return jax.shard_map(
        functools.partial(shards, mesh.shape["row"], mesh.shape["col"]),
        mesh=mesh,
        in_specs=placed,
        out_specs=(P("col"), P("col", "row"), P("row", "col"), P("row", "col"), P("col", "row")),
        check_vma=False,
    )
```
